128 devices in a mesh: dp: 8 (over x, core), adapter: 16 (over z, y).
Axes of the slice: x: 4, y: 4, z: 4, core: 2. Of those that a mesh axis runs over, the one named last changes fastest.
Arguments:
- residual_input: bfloat16 [65536, 2560], P(('dp', 'adapter')), may hold values from -6 to 6
- input_norm_gain: float32 [2560], replicated, may hold values from 0.5 to 1.5
- base_projection_weight: bfloat16 [2560, 4096], P('adapter', 'dp'), may hold values from -0.125 to 0.125
- query_key_gains: float32 [2, 256], replicated, may hold values from 0.5 to 1.5
- adapter_down_weight: bfloat16 [64, 2560, 48], P('adapter'), may hold values from -0.125 to 0.125
- adapter_up_weight: bfloat16 [64, 16, 4096], P('adapter'), may hold values from -1.5 to 1.5
- row_adapter_index: int32 [65536, 1], P(('dp', 'adapter')), may hold values from 0 to 63; in each aligned block of 512 rows (0 to 511, 512 to 1023, ...) at most 16 rows name the same one
- row_sequence_index: int32 [65536], P(('dp', 'adapter')), may hold values from 0 to 7, never falling along the last dimension, each value on 1 to 12288 neighbouring positions
Outputs:
- attended: bfloat16 [65536, 2048], P(('dp', 'adapter'))
The draws below stay inside these ranges and needn't reach their ends.
Inputs may be any that keep to these rules, and one draw needn't show every extreme that they name: `row_adapter_index`: among the rows of one device, no adapter serves more than 16 rows; some adapter serves exactly 16 rows of some device. `row_sequence_index`: sequence numbers never fall along the rows; every sequence has 1 to 12288 rows, one exactly 12288.
All inputs are finite; a program needn't handle non-finite values.
Results may differ from the reference program's by a relative error of at most 0.02.
Values may be sent and summed in bfloat16 or wider, within the bound.
A program may use at most 128 MiB of HBM per device.

```python
import math
import jax
import jax.numpy as jnp
import numpy as np
from jax import lax

MODEL_WIDTH = 2560
HEADS = 8
KV_HEADS = 4
HEAD_DIM = 256
WINDOW = 1024
ADAPTER_RANK = 16
TOK_DEV = 512
PROJECTED_WIDTH = 4096
ADAPTER_TOTAL = 64
PACKED_ROWS = 65536
CAP = 16
SEG_COUNT = 8
SEG_MAX = 12288


def shard_levels(rng, shape, shards, smallest, largest):
    def one(position, shards_of):
        steps = jax.random.uniform(jax.random.fold_in(jax.random.fold_in(rng, 6), position), (shards_of,), jnp.float32, smallest / len(shards), largest / len(shards))
        return jnp.repeat(jnp.exp(steps), shape[position] // shards_of).reshape((-1,) + (1,) * (len(shape) - position - 1))

    factor_of = one(*shards[0])
    for cut in shards[1:]:
        factor_of = factor_of * one(*cut)
    return factor_of


def profile(count, total, reach, skew):
    loads = [(1 << 20) // math.isqrt(grade ** skew) + 1 for grade in range(2, count + 1)]
    spare, counts = total - reach - (count - 1), [1] * (count - 1)
    while spare > 0:
        candidates = [i for i in range(count - 1) if counts[i] < reach]
        whole, budget = sum([loads[i] for i in candidates]), spare
        for i in candidates:
            more = min(reach - counts[i], max(1, budget * loads[i] // whole), spare)
            counts[i] = counts[i] + more
            spare = spare - more
    return np.array([reach] + counts)


def ragged(stream_key, number_of, total, reach, slope):
    if number_of == 2:
        one = jax.random.randint(stream_key, (), max(1, total - reach), min(reach, total - 1) + 1)
        return jnp.stack([one, total - one])
    tallies = jnp.asarray(profile(number_of, total, reach, slope), jnp.int32)
    couples = (number_of - 1) // 2
    source_of, sink = tallies[1:1 + 2 * couples:2], tallies[2:2 + 2 * couples:2]
    margin = jnp.minimum(source_of - 1, reach - sink)
    passed = jax.random.randint(jax.random.fold_in(stream_key, 1), (couples,), 0, 1 << 20) % (margin + 1)
    tallies = tallies.at[1:1 + 2 * couples:2].set(source_of - passed).at[2:2 + 2 * couples:2].set(sink + passed)
    return tallies[jax.random.permutation(jax.random.fold_in(stream_key, 2), number_of)]


def shared_out(rng, own, number, rows, number_of, top, bound, slope):
    ranking = jax.random.permutation(rng, number_of)
    crowded, ordinary = load_shares(number_of, rows * top, bound, slope, True), load_shares(number_of, rows * top, bound, slope, False)
    places = jnp.arange(number_of)

    def named(lengths, turn):
        used = int((lengths > 0).sum())
        fixed = max(1, used // 4)
        shifted = fixed + (places - fixed + turn * (used - fixed)) % max(1, number_of - fixed)
        return jnp.zeros((number_of,), jnp.int32).at[ranking[jnp.where(places < fixed, places, shifted)]].set(jnp.asarray(lengths, jnp.int32))

    lengths = jnp.where(number % 4 == 0, named(crowded, number // 4), named(ordinary, number - number // 4 - 1))
    mixed = jax.random.permutation(jax.random.fold_in(own, 3), number_of)
    giver, taker = mixed[0:number_of // 2 * 2:2], mixed[1:number_of // 2 * 2:2]
    room = jnp.minimum(lengths[giver] - 1, bound - lengths[taker]) // 2
    room = jnp.where((giver == ranking[0]) | (taker == ranking[0]) | (lengths[taker] == 0), 0, jnp.maximum(room, 0))
    shifted = jax.random.randint(jax.random.fold_in(own, 4), (number_of // 2,), 0, 1 << 20) % (room + 1)
    lengths = lengths.at[giver].add(-shifted).at[taker].add(shifted)
    labels = jnp.searchsorted(jnp.cumsum(lengths), jnp.arange(rows * top), side="right").astype(jnp.int32)
    grid = labels.reshape(top, rows).T
    grid = grid[jax.random.permutation(jax.random.fold_in(own, 1), rows)]
    turn = jax.random.randint(jax.random.fold_in(own, 2), (rows, 1), 0, top)
    return jnp.take_along_axis(grid, (jnp.arange(top)[None, :] + turn) % top, axis=1)


def load_shares(amount, total, most, skew, full):
    loads = [(1 << 20) // math.isqrt(rank ** skew) + 1 for rank in range(1, amount + 1)]
    largest = most if full else min(most, max(-(-total // amount), total * loads[0] // sum(loads)))
    least = 1 if total - largest >= amount - 1 else 0
    holding, spare = [largest] + [least] * (amount - 1), total - largest - least * (amount - 1)
    while spare > 0:
        free = [i for i in range(1, amount) if holding[i] < largest] or [i for i in range(1, amount) if holding[i] < most]
        whole, left = sum([loads[i] for i in free]), spare
        for i in free:
            extra = min(most - holding[i], max(1, left * loads[i] // whole), spare)
            holding[i] = holding[i] + extra
            spare = spare - extra
    return np.array(holding)


def gaussian(rng, shape, spread, limit, cuts=(), held_as=jnp.bfloat16):
    array = spread * jax.random.normal(rng, shape, jnp.float32)
    if cuts:
        array = array * shard_levels(rng, shape, cuts, -0.22, 0.18)
    return jnp.clip(array, -limit, limit).astype(held_as)


def setup_inputs(seed: int = 0) -> dict:
    streams_of = jax.random.split(jax.random.key(seed), 9)
    residual_input = gaussian(streams_of[0], (PACKED_ROWS, MODEL_WIDTH), 1.0, 6.0, ((0, 128),))
    input_norm_gain = jnp.clip(1.0 + 0.1 * jax.random.normal(streams_of[1], (MODEL_WIDTH,), jnp.float32), 0.5, 1.5)
    base_projection_weight = gaussian(streams_of[2], (MODEL_WIDTH, PROJECTED_WIDTH), MODEL_WIDTH ** -0.5, 0.125, ((0, 16), (1, 8)))
    query_key_gains = jnp.clip(1.0 + 0.1 * jax.random.normal(streams_of[3], (2, HEAD_DIM), jnp.float32), 0.5, 1.5)
    adapter_down_weight = gaussian(streams_of[4], (ADAPTER_TOTAL, MODEL_WIDTH, 3 * ADAPTER_RANK), MODEL_WIDTH ** -0.5, 0.125, ((0, 16),))
    adapter_up_weight = gaussian(streams_of[5], (ADAPTER_TOTAL, ADAPTER_RANK, PROJECTED_WIDTH), ADAPTER_RANK ** -0.5, 1.5, ((0, 16),))
    row_adapter_index_keys = jax.random.split(jax.random.fold_in(streams_of[6], 1), PACKED_ROWS // TOK_DEV)
    row_adapter_index_turns = jax.random.permutation(jax.random.fold_in(streams_of[6], 3), PACKED_ROWS // TOK_DEV)
    row_adapter_index = jax.vmap(lambda own, number: shared_out(jax.random.fold_in(streams_of[6], 2), own, number, TOK_DEV, ADAPTER_TOTAL, 1, CAP, 2))(row_adapter_index_keys, row_adapter_index_turns).reshape((PACKED_ROWS, 1))
    row_sequence_index = jnp.searchsorted(jnp.cumsum(ragged(streams_of[7], SEG_COUNT, PACKED_ROWS, SEG_MAX, 2)), jnp.arange(PACKED_ROWS), side="right").astype(jnp.int32)
    return {"residual_input": residual_input, "input_norm_gain": input_norm_gain, "base_projection_weight": base_projection_weight, "query_key_gains": query_key_gains, "adapter_down_weight": adapter_down_weight, "adapter_up_weight": adapter_up_weight, "row_adapter_index": row_adapter_index, "row_sequence_index": row_sequence_index}


def head_norm(block, heads, gain):
    shaped = block.reshape(block.shape[0], heads, HEAD_DIM)
    scaled = shaped * lax.rsqrt(lax.optimization_barrier(jnp.mean(shaped * shaped, axis=-1, keepdims=True)) + 1e-06) * gain
    return scaled.astype(jnp.bfloat16)

def reference(residual_input, input_norm_gain, base_projection_weight, query_key_gains, adapter_down_weight, adapter_up_weight, row_adapter_index, row_sequence_index):
    width_q = HEADS * HEAD_DIM
    width_k = KV_HEADS * HEAD_DIM
    group = HEADS // KV_HEADS
    before = (WINDOW + TOK_DEV - 2) // TOK_DEV
    span = (before + 1) * TOK_DEV
    block_list = PACKED_ROWS // TOK_DEV
    values_in = residual_input.astype(jnp.float32)
    normed = (values_in * lax.rsqrt(lax.optimization_barrier(jnp.mean(values_in * values_in, axis=-1, keepdims=True)) + 1e-06) * input_norm_gain).astype(jnp.bfloat16)
    base = jnp.dot(normed, base_projection_weight, preferred_element_type=jnp.float32).astype(jnp.bfloat16)
    adapter_ids = row_adapter_index[:, 0].astype(jnp.int32)

    def adapter_block(adapter_index):
        start = (adapter_index * TOK_DEV).astype(jnp.int32)
        rows = lax.dynamic_slice_in_dim(normed, start, TOK_DEV, 0).astype(jnp.float32)
        chosen_adapter = lax.dynamic_slice_in_dim(adapter_ids, start, TOK_DEV, 0)
        down_projected_rows = jnp.take(adapter_down_weight, chosen_adapter, axis=0).astype(jnp.float32)
        rank_values = jnp.einsum('td,tdr->tr', rows, down_projected_rows).astype(jnp.bfloat16)
        rank_values = lax.optimization_barrier(rank_values).astype(jnp.float32)
        up_projected_rows = jnp.take(adapter_up_weight, chosen_adapter, axis=0).astype(jnp.float32)
        part_q = jnp.einsum('tr,trq->tq', rank_values[:, 0:ADAPTER_RANK], up_projected_rows[:, :, 0:width_q])
        part_k = jnp.einsum('tr,trq->tq', rank_values[:, ADAPTER_RANK:2 * ADAPTER_RANK], up_projected_rows[:, :, width_q:width_q + width_k])
        part_v = jnp.einsum('tr,trq->tq', rank_values[:, 2 * ADAPTER_RANK:3 * ADAPTER_RANK], up_projected_rows[:, :, width_q + width_k:])
        return jnp.concatenate([part_q, part_k, part_v], axis=1).astype(jnp.bfloat16)
    delta_update = lax.map(adapter_block, jnp.arange(block_list, dtype=jnp.int32)).reshape(PACKED_ROWS, PROJECTED_WIDTH)
    projected = base.astype(jnp.float32) + delta_update.astype(jnp.float32)
    queries = head_norm(projected[:, 0:width_q], HEADS, query_key_gains[0])
    keys = head_norm(projected[:, width_q:width_q + width_k], KV_HEADS, query_key_gains[1])
    values = projected[:, width_q + width_k:].astype(jnp.bfloat16).reshape(PACKED_ROWS, KV_HEADS, HEAD_DIM)
    pad = before * TOK_DEV
    keys_pad = jnp.concatenate([jnp.zeros((pad, KV_HEADS, HEAD_DIM), jnp.bfloat16), keys], axis=0)
    values_pad = jnp.concatenate([jnp.zeros((pad, KV_HEADS, HEAD_DIM), jnp.bfloat16), values], axis=0)
    seg_pad = jnp.concatenate([jnp.full((pad,), -1, jnp.int32), row_sequence_index.astype(jnp.int32)], axis=0)

    def attend_block(adapter_index):
        start = (adapter_index * TOK_DEV).astype(jnp.int32)
        query_block = lax.dynamic_slice_in_dim(queries, start, TOK_DEV, 0).reshape(TOK_DEV, KV_HEADS, group, HEAD_DIM)
        query_seg = lax.dynamic_slice_in_dim(row_sequence_index.astype(jnp.int32), start, TOK_DEV, 0)
        key_block = lax.dynamic_slice_in_dim(keys_pad, start, span, 0)
        value_block = lax.dynamic_slice_in_dim(values_pad, start, span, 0)
        key_seg = lax.dynamic_slice_in_dim(seg_pad, start, span, 0)
        query_pos = start + jnp.arange(TOK_DEV, dtype=jnp.int32)
        key_pos = start - pad + jnp.arange(span, dtype=jnp.int32)
        gap = query_pos[:, None] - key_pos[None, :]
        allowed = (query_seg[:, None] == key_seg[None, :]) & (gap >= 0) & (gap < WINDOW) & (key_pos[None, :] >= 0)
        scores = jnp.einsum('tkgd,skd->kgts', query_block.astype(jnp.float32), key_block.astype(jnp.float32)) * HEAD_DIM ** (-0.5)
        weights = jnp.where(allowed[None, None], jnp.exp(scores), jnp.float32(0.0))
        total = lax.optimization_barrier(jnp.sum(weights, axis=-1))
        probs = weights.astype(jnp.bfloat16)
        summed = jnp.einsum('kgts,skd->tkgd', probs.astype(jnp.float32), value_block.astype(jnp.float32))
        result = summed / jnp.transpose(total, (2, 0, 1))[..., None]
        return result.reshape(TOK_DEV, width_q).astype(jnp.bfloat16)
    return lax.map(attend_block, jnp.arange(block_list, dtype=jnp.int32)).reshape(PACKED_ROWS, width_q)
```

```python
import jax
import jax.numpy as jnp
import numpy as np
from jax import lax
from jax.experimental import pallas as pl
from jax.experimental.pallas import tpu as pltpu
from jax.sharding import PartitionSpec as P

HEADS = 8
KV_HEADS = 4
HEAD_DIM = 256
ROWS = 512
WIDTH = 2560
BF16 = jnp.bfloat16
F32 = jnp.float32


def dot(a, b, dims=((1,), (0,))):
    return lax.dot_general(a, b, (dims, ((), ())), preferred_element_type=F32)


def kernel(
    x_ref, g_ref, gains_ref, ids_ref, fold_ref, tile_ref, cols_ref, w_ref, d_ref, u_ref,
    out_ref,
    xg, wu, dn, rpt, qs, kall, vall, ob, ids, hids, acol, scol, krow,
    sh_send, d_sem, u_sem, w_sem, x_send, x_recv, f_send, i_send, i_recv,
    g_send, g_recv, r_send, r_recv, h_send, h_recv, o_send, o_recv,
):
    dp = lax.axis_index("dp")
    ad = lax.axis_index("adapter")
    x, c = dp // 2, dp % 2
    z, y = ad // 4, ad % 4
    g, yl = y // 2, y % 2

    def dev(x_, c_, z_, y_):
        return (x_ * 2 + c_, z_ * 4 + y_)

    def half_of(y_):
        return ((y_ + 1) // 2) % 2

    def remote(src, dst, ssem, rsem, to):
        return pltpu.make_async_remote_copy(
            src_ref=src, dst_ref=dst, send_sem=ssem, recv_sem=rsem,
            device_id=to, device_id_type=pl.DeviceIdType.MESH,
        )

    def arrived(ref, sem):
        pltpu.make_async_copy(ref, ref, sem).wait()

    half = half_of(y)
    kv = c + 2 * half
    ypar = 1 - 2 * yl + y
    sib = dev(x, 1 - c, z, y)
    mate = dev(x, c, z, ypar)
    diag = dev(x, 1 - c, z, ypar)
    xbit = x // 2
    b = (1 - xbit) * (x % 2) + xbit * c
    px = (1 - xbit) * (1 - x) + xbit * x
    pc = (1 - xbit) * c + xbit * (1 - c)
    up_x, dn_x = (x + 1) % 4, (x + 3) % 4
    up_z, dn_z = (z + 1) % 4, (z + 3) % 4
    y3 = 3 - y
    wrap = g * (z // 3)
    tz = (z + g) % 4
    swrap = (1 - g) * ((3 - z) // 3)
    sz = (z + 3 + g) % 4
    halo_to = [dev(x, c, tz, y3), dev((x + wrap) % 4, c, tz, y3)]
    halo_from = [dev((x + 4 - swrap) % 4, c, sz, y3), dev(x, c, sz, y3)]
    slot_of = [wrap, 1 - wrap]

    barrier = pltpu.get_barrier_semaphore()
    partners = [sib, mate, diag]
    partners += [dev(x, c, z, (y + k) % 4) for k in (1, 2, 3)]
    partners += [dev(px, pc, z, k) for k in range(4)]
    partners += [dev(up_x, c, z, y), dev(dn_x, c, z, y), dev(x, c, up_z, y), dev(x, c, dn_z, y)]
    partners += halo_to + halo_from
    for to in partners:
        pl.semaphore_signal(barrier, inc=1, device_id=to, device_id_type=pl.DeviceIdType.MESH)
    pl.semaphore_wait(barrier, len(partners))

    pending = []

    def go(copy):
        copy.start()
        pending.append(copy)
        return copy

    y2 = (y + 2) % 4
    dsrc = d_ref.at[pl.ds(pl.multiple_of(96 * c, 32), 96), pl.ds(pl.multiple_of(640 * x, 128), 640)]
    ddst = dn.at[z, pl.ds(pl.multiple_of(96 * g, 32), 96), pl.ds(pl.multiple_of(640 * x, 128), 640)]
    dloc = pltpu.make_async_copy(dsrc, ddst, d_sem.at[0])
    dloc.start()
    dsend = go(remote(dsrc, ddst, sh_send.at[0], d_sem.at[1], dev(x, c, z, y2)))

    def up_src(y_):
        kv_ = c + 2 * half_of(y_)
        col = (1 - xbit) * (kv_ * 512 + x * 256) + xbit * (2048 + (x - 2) * 1024 + kv_ * 256)
        return u_ref.at[:, pl.ds(pl.multiple_of(col, 128), 256)]

    udst = wu.at[x, z, pl.ds(pl.multiple_of(640 + 64 * y, 64), 64), :]
    for k in (1, 2, 3):
        yt = (y + k) % 4
        go(remote(up_src(yt), udst, sh_send.at[k], u_sem.at[y], dev(x, c, z, yt)))
    pltpu.make_async_copy(up_src(y), udst, u_sem.at[y]).start()
    kept = w_ref.at[:, pl.ds(pl.multiple_of(b * 256, 256), 256)]
    other = w_ref.at[:, pl.ds(pl.multiple_of((1 - b) * 256, 256), 256)]
    wrows = pl.ds(pl.multiple_of(160 * y, 32), 160)
    kept_sends = []
    for k, yt in enumerate((b, 3 - b)):
        send = remote(kept, wu.at[x, z, wrows, :], sh_send.at[4 + k], w_sem.at[y], dev(x, c, z, yt))
        kept_sends.append((yt, send))

        @pl.when(yt == y)
        def _():
            pltpu.make_async_copy(kept, wu.at[x, z, wrows, :], w_sem.at[y]).start()

        @pl.when(yt != y)
        def _():
            send.start()

        go(remote(other, wu.at[px, z, wrows, :], sh_send.at[6 + k], w_sem.at[y], dev(px, pc, z, yt)))

    own = 2 * c + yl
    iloc = pltpu.make_async_copy(ids_ref, ids.at[own], i_recv.at[own])
    iloc.start()
    for k, to in enumerate((sib, mate, diag)):
        go(remote(ids_ref, ids.at[own], i_send.at[k], i_recv.at[own], to))
    for k in range(4):
        val = x_ref[k * 128 : (k + 1) * 128, :].astype(F32)
        scale = lax.rsqrt(jnp.mean(val * val, axis=-1, keepdims=True) + 1e-06)
        rows = pl.ds(pl.multiple_of(own * 512 + k * 128, 128), 128)
        xg[rows, :] = (val * scale * g_ref[...]).astype(BF16)
        go(remote(xg.at[rows, :], xg.at[rows, :], x_send.at[0, k], x_recv.at[0, k], mate))
        go(remote(xg.at[rows, :], xg.at[rows, :], x_send.at[1, k], x_recv.at[1, k], sib))

    def block_rows(blk, k):
        return xg.at[pl.ds(pl.multiple_of(blk * 512 + k * 128, 128), 128), :]

    def slot(part, stage, i, lo, n):
        if part < 2:
            rows = pl.ds(part * 96 + lo, n)
            cols_i = pl.ds(pl.multiple_of(i * 640, 128), 640)
            cols_x = pl.ds(pl.multiple_of(x * 640, 128), 640)
            if part == 0:
                return dn.at[z, rows, cols_i] if stage == 0 else dn.at[i, rows, :]
            return dn.at[i, rows, cols_x] if stage == 0 else dn.at[:, rows, cols_i]
        rows = pl.ds((part - 2) * 448 + lo, n)
        if part == 2:
            return wu.at[i, z, rows, :] if stage == 0 else wu.at[:, i, rows, :]
        return wu.at[x, i, rows, :] if stage == 0 else wu.at[i, :, rows, :]

    def step(part, s):
        size = 96 if part < 2 else 448
        stage = s // 2
        along_x = (part % 2 == 0) == (stage == 0)
        me, up, dw = (x, up_x, dn_x) if along_x else (z, up_z, dn_z)
        to_up = dev(up, c, z, y) if along_x else dev(x, c, up, y)
        to_dn = dev(dw, c, z, y) if along_x else dev(x, c, dw, y)
        copies = []
        for way, to in enumerate((to_up, to_dn)):
            if s % 2 == 0:
                ref = slot(part, stage, me, 0, size)
            else:
                ref = slot(part, stage, dw if way == 0 else up, way * (size // 2), size // 2)
            copies.append(
                go(remote(ref, ref, g_send.at[part, s, way], g_recv.at[part, s, way], to))
            )
        return copies

    def done(copies):
        for copy in copies:
            copy.wait_recv()

    dloc.wait()
    dsend.wait_recv()
    d1, d2 = step(0, 0), step(1, 0)
    for k in range(4):
        arrived(wu.at[x, z, pl.ds(640 + 64 * k, 64), :], u_sem.at[k])
        arrived(wu.at[x, z, pl.ds(160 * k, 160), :], w_sem.at[k])
    w1, w2 = step(2, 0), step(3, 0)
    done(d1), done(d2)
    d1, d2 = step(0, 1), step(1, 1)
    done(d1), done(d2)
    d1, d2 = step(0, 2), step(1, 2)
    done(w1), done(w2)
    w1, w2 = step(2, 1), step(3, 1)
    done(d1), done(d2)
    d1, d2 = step(0, 3), step(1, 3)
    done(w1), done(w2)
    w1, w2 = step(2, 2), step(3, 2)

    for k in range(4):
        arrived(ids.at[k], i_recv.at[k])
    for blk in range(4):
        for k in range(4):
            at = slice(blk * 512 + k * 128, blk * 512 + (k + 1) * 128)
            acol[at, :] = jnp.broadcast_to(ids[blk, k : k + 1, :], (128, 128)).T
            scol[at, :] = jnp.broadcast_to(ids[blk, 4 + k : 5 + k, :], (128, 128)).T
    for r in range(2):
        ref = ids.at[2 * r : 2 * r + 2]
        go(remote(ref, hids.at[slot_of[r]], h_send.at[8 + r], h_recv.at[slot_of[r], 4], halo_to[r]))
    for k in range(4):
        arrived(block_rows(0, 0), x_recv.at[1, k])

    done(d1), done(d2)

    def ranks(o):
        blk = ((c + o) % 2) * 2 + (yl + o // 2) % 2
        rows = pl.ds(pl.multiple_of(blk * 512, 512), 512)
        vals = jnp.concatenate(
            [dot(xg[rows, :], dn[k], ((1,), (1,))).astype(BF16) for k in range(4)], axis=1
        )
        first = (c * 2 + yl * 4).astype(F32)
        mine = acol[rows, 0:1] == cols_ref[0:1, :] + first
        kept_vals = jnp.where(mine, vals.astype(F32), 0.0).astype(BF16)
        rpt[own, :, rows] = dot(fold_ref[...], kept_vals, ((1,), (1,))).astype(BF16)
        for k, to in enumerate((sib, mate, diag)):
            ref = rpt.at[own, :, rows]
            remote(ref, ref, r_send.at[k, o], r_recv.at[own, blk], to).start()

    def two_ranks(first):
        def run(o, carry):
            ranks(o)
            return carry

        lax.fori_loop(first, first + 2, run, 0)

    two_ranks(0)
    done(w1), done(w2)
    w1, w2 = step(2, 3), step(3, 3)
    forwards = []
    mblk = 2 * c + 1 - yl
    for k in range(4):
        arrived(block_rows(0, 0), x_recv.at[0, k])
        ref = block_rows(mblk, k)
        forwards.append(go(remote(ref, ref, f_send.at[k], x_recv.at[2, k], sib)))
    done(forwards)
    two_ranks(2)
    done(w1), done(w2)

    lane = lax.broadcasted_iota(jnp.int32, (1, 128), 1)
    lane_adapter = (lane // 16).astype(F32)

    def halo_copies(blk, o):
        r, part = blk // 2, blk % 2
        src = pl.ds(pl.multiple_of(1024 + part * 512, 512), 512)
        dst = pl.ds(pl.multiple_of(part * 512, 512), 512)
        sl = (r + wrap) % 2
        to = dev((x + wrap * r) % 4, c, tz, y3)
        return [
            remote(buf.at[r, src, :], buf.at[sl, dst, :], h_send.at[2 * o + n],
                   h_recv.at[sl, part * 2 + n], to)
            for n, buf in enumerate((kall, vall))
        ]

    def project(o, carry):
        blk = ((c + o) % 2) * 2 + (yl + o // 2) % 2
        for k in range(1, 4):
            src = (own + k) % 4
            arrived(rpt.at[src, :, pl.ds(0, 512)], r_recv.at[src, blk])
        rows = pl.ds(pl.multiple_of(blk * 512, 512), 512)
        total_ranks = rpt[0, :, rows].astype(F32)
        for k in range(1, 4):
            total_ranks = total_ranks + rpt[k, :, rows].astype(F32)
        tiled = dot(total_ranks.T.astype(BF16), tile_ref[...])
        adapters = acol[rows, :]
        for part, col_blocks in enumerate(((0, 1), (2,), (3,))):
            mine = tiled[:, part * 128 : (part + 1) * 128]
            spread = [
                jnp.where(adapters == lane_adapter + 8.0 * n, mine, 0.0).astype(BF16)
                for n in range(8)
            ]
            for cb in col_blocks:
                base = jnp.zeros((512, 256), F32)
                delta = jnp.zeros((512, 256), F32)
                for k in range(4):
                    base = base + dot(xg[rows, k * 640 : (k + 1) * 640], wu[cb, k, 0:640, :])
                    pair = jnp.concatenate([spread[2 * k], spread[2 * k + 1]], axis=1)
                    delta = delta + dot(pair, wu[cb, k, 640:896, :])
                proj = base.astype(BF16).astype(F32) + delta.astype(BF16).astype(F32)
                if cb < 3:
                    scale = lax.rsqrt(jnp.mean(proj * proj, axis=-1, keepdims=True) + 1e-06)
                    gain = gains_ref[0:1, :] if cb < 2 else gains_ref[1:2, :]
                    proj = proj * scale * gain
                val = proj.astype(BF16)
                at = pl.ds(pl.multiple_of(1024 + (blk % 2) * 512, 512), 512)
                if cb < 2:
                    qs[cb, rows, :] = val * BF16(0.0625)
                elif cb == 2:
                    kall[blk // 2, at, :] = val
                else:
                    vall[blk // 2, at, :] = val
        for copy in halo_copies(blk, o):
            copy.start()
        return carry

    lax.fori_loop(0, 4, project, 0)

    for sl in range(2):
        arrived(hids.at[sl], h_recv.at[sl, 4])
    nothing = jnp.where(x * 8 + z * 2 + g == 0, 1.0, 0.0).astype(F32)
    for r in range(2):
        for t in range(8):
            blk, k = (t % 4) // 2, (t % 2) * 2
            if t < 4:
                pair = [hids[r, blk, 4 + k + n : 5 + k + n, :] for n in range(2)]
                if r == 0:
                    pair = [p - nothing * (p + 1.0) for p in pair]
            else:
                pair = [ids[2 * r + blk, 4 + k + n : 5 + k + n, :] for n in range(2)]
            krow[r, t] = jnp.broadcast_to(jnp.concatenate(pair, axis=1), (8, 256))

    ahead = lax.broadcasted_iota(jnp.int32, (256, 256), 0) - lax.broadcasted_iota(
        jnp.int32, (256, 256), 1
    )

    def out_copy(blk):
        src = ob.at[pl.ds(pl.multiple_of(blk * 512, 512), 512), :]
        dst = out_ref.at[:, pl.ds(pl.multiple_of(kv * 512, 512), 512)]
        return src, dst, dev(x, blk // 2, z, g * 2 + blk % 2)

    def attend(n, carry):
        r, i = n // 4, n % 4
        for h in range(2):
            rows = pl.ds(pl.multiple_of(n * 256, 256), 256)
            q = qs[h, rows, :]
            sq = scol[rows, 0:1]
            acc = jnp.zeros((256, 256), F32)
            total = jnp.zeros((256, 128), F32)
            for j in range(5):
                keys = pl.ds(pl.multiple_of((i + j) * 256, 256), 256)
                s = dot(q, kall[r, keys, :], ((1,), (1,)))
                ok = sq == krow[r, i + j, 0:1, :]
                if j == 0:
                    ok = ok & (ahead < 0)
                if j == 4:
                    ok = ok & (ahead >= 0)
                w = jnp.where(ok, jnp.exp(s), 0.0)
                total = total + w[:, 0:128] + w[:, 128:256]
                acc = acc + dot(w.astype(BF16), vall[r, keys, :])
            norm = jnp.sum(total, axis=-1, keepdims=True)
            ob[rows, h * 256 : (h + 1) * 256] = (acc / norm).astype(BF16)

        @pl.when(n % 2 == 1)
        def _():
            blk = n // 2
            src, dst, to = out_copy(blk)

            @pl.when(blk == own)
            def _():
                pltpu.make_async_copy(src, dst, o_recv.at[own]).start()

            @pl.when(blk != own)
            def _():
                remote(src, dst, o_send.at[blk], o_recv.at[own], to).start()

        return carry

    for r in range(2):
        for k in range(4):
            arrived(kall.at[r, pl.ds(0, 512), :], h_recv.at[r, k])
        lax.fori_loop(4 * r, 4 * r + 4, attend, 0)

    for k in range(4):
        arrived(out_ref.at[:, pl.ds(0, 512)], o_recv.at[k])
    for k in range(1, 4):
        blk = (own + k) % 4
        src, dst, to = out_copy(blk)
        remote(src, dst, o_send.at[blk], o_recv.at[own], to).wait_send()
    for o in range(4):
        for k, to in enumerate((sib, mate, diag)):
            ref = rpt.at[own, :, pl.ds(0, 512)]
            remote(ref, ref, r_send.at[k, o], r_recv.at[own, o], to).wait_send()
        blk = ((c + o) % 2) * 2 + (yl + o // 2) % 2
        for copy in halo_copies(blk, o):
            copy.wait_send()
    for yt, send in kept_sends:

        @pl.when(yt != y)
        def _():
            send.wait_send()

    for copy in pending:
        copy.wait_send()


FOLD = np.zeros((48, 768), np.float32)
FOLD[np.arange(768) % 48, np.arange(768)] = 1.0
TILE = np.zeros((48, 384), np.float32)
for _lane in range(384):
    TILE[(_lane // 128) * 16 + _lane % 16, _lane] = 1.0
_c = np.arange(768)
COLS = np.tile(((_c // 192) * 16 + (_c % 192 // 96) * 8 + _c % 96 // 48).astype(np.float32), (8, 1))


def body(
    residual_input,
    input_norm_gain,
    base_projection_weight,
    query_key_gains,
    adapter_down_weight,
    adapter_up_weight,
    row_adapter_index,
    row_sequence_index,
):
    ids = jnp.concatenate(
        [row_adapter_index.reshape(4, 128), row_sequence_index.reshape(4, 128)], axis=0
    ).astype(F32)
    down = jnp.transpose(adapter_down_weight, (0, 2, 1)).reshape(192, WIDTH)
    up = adapter_up_weight.reshape(64, 4096)
    vm = pl.BlockSpec(memory_space=pltpu.VMEM)
    anyspace = pl.BlockSpec(memory_space=pl.ANY)
    dma = pltpu.SemaphoreType.DMA
    return pl.pallas_call(
        kernel,
        out_shape=jax.ShapeDtypeStruct((ROWS, HEADS * HEAD_DIM), BF16),
        in_specs=[vm] * 7 + [anyspace] * 3,
        out_specs=anyspace,
        scratch_shapes=[
            pltpu.VMEM((2048, WIDTH), BF16),
            pltpu.VMEM((4, 4, 896, 256), BF16),
            pltpu.VMEM((4, 192, WIDTH), BF16),
            pltpu.VMEM((4, 48, 2048), BF16),
            pltpu.VMEM((2, 2048, 256), BF16),
            pltpu.VMEM((2, 2048, 256), BF16),
            pltpu.VMEM((2, 2048, 256), BF16),
            pltpu.VMEM((2048, 512), BF16),
            pltpu.VMEM((4, 8, 128), F32),
            pltpu.VMEM((2, 2, 8, 128), F32),
            pltpu.VMEM((2048, 128), F32),
            pltpu.VMEM((2048, 128), F32),
            pltpu.VMEM((2, 8, 8, 256), F32),
            dma((8,)), dma((2,)), dma((4,)), dma((4,)),
            dma((2, 4)), dma((3, 4)), dma((4,)),
            dma((3,)), dma((4,)),
            dma((4, 4, 2)), dma((4, 4, 2)),
            dma((3, 4)), dma((4, 4)),
            dma((10,)), dma((2, 5)),
            dma((4,)), dma((4,)),
        ],
        compiler_params=pltpu.CompilerParams(
            collective_id=0, has_side_effects=True, vmem_limit_bytes=60 << 20
        ),
        name="block",
    )(
        residual_input,
        input_norm_gain.reshape(1, WIDTH),
        query_key_gains,
        ids,
        jnp.asarray(FOLD, BF16),
        jnp.asarray(TILE, BF16),
        jnp.asarray(COLS),
        base_projection_weight,
        down,
        up,
    )


def solution(mesh):
    placed = (
        P(("dp", "adapter"), None),
        P(),
        P("adapter", "dp"),
        P(),
        P("adapter", None, None),
        P("adapter", None, None),
        P(("dp", "adapter"), None),
        P(("dp", "adapter")),
    )
    return jax.shard_map(
        body, mesh=mesh, in_specs=placed, out_specs=P(("dp", "adapter"), None), check_vma=False
    )
```

```python
import jax
import jax.numpy as jnp
import numpy as np
from jax import lax
from jax.experimental import pallas as pl
from jax.experimental.pallas import tpu as pltpu
from jax.sharding import PartitionSpec as P

HEADS = 8
KV_HEADS = 4
HEAD_DIM = 256
ROWS = 512
WIDTH = 2560
BF16 = jnp.bfloat16
F32 = jnp.float32


def dot(a, b, dims=((1,), (0,))):
    return lax.dot_general(a, b, (dims, ((), ())), preferred_element_type=F32)


def kernel(
    x_ref, g_ref, gains_ref, ids_ref, fold_ref, tile_ref, cols_ref, w_ref, d_ref, u_ref,
    out_ref,
    xg, wb, ub, dn, rpt, qs, kall, vall, ob, acc_ref, tot_ref, ids, hids, acol, scol, krow,
    d_send, d_sem, u_send, u_sem, w_send, w_sem, x_send, x_recv, f_send, i_send, i_recv,
    g_send, g_recv, r_send, r_recv, h_send, h_recv, o_send, o_recv,
):
    dp = lax.axis_index("dp")
    ad = lax.axis_index("adapter")
    x, c = dp // 2, dp % 2
    z, y = ad // 4, ad % 4
    g, yl = y // 2, y % 2

    def dev(x_, c_, z_, y_):
        return (x_ * 2 + c_, z_ * 4 + y_)

    def half_of(y_):
        return ((y_ + 1) // 2) % 2

    def remote(src, dst, ssem, rsem, to):
        return pltpu.make_async_remote_copy(
            src_ref=src, dst_ref=dst, send_sem=ssem, recv_sem=rsem,
            device_id=to, device_id_type=pl.DeviceIdType.MESH,
        )

    def arrived(ref, sem):
        pltpu.make_async_copy(ref, ref, sem).wait()

    half = half_of(y)
    kv = c + 2 * half
    ypar = 1 - 2 * yl + y
    sib = dev(x, 1 - c, z, y)
    mate = dev(x, c, z, ypar)
    diag = dev(x, 1 - c, z, ypar)
    xbit = x // 2
    hb = (1 - xbit) * (x % 2) + xbit * c
    up_x, dn_x = (x + 1) % 4, (x + 3) % 4
    up_z, dn_z = (z + 1) % 4, (z + 3) % 4
    y3 = 3 - y
    twin = dev(x, c, z, y3)
    wrap = g * (z // 3)
    tz = (z + g) % 4
    swrap = (1 - g) * ((3 - z) // 3)
    sz = (z + 3 + g) % 4
    halo_to = [dev(x, c, tz, y3), dev((x + wrap) % 4, c, tz, y3)]
    halo_from = [dev((x + 4 - swrap) % 4, c, sz, y3), dev(x, c, sz, y3)]
    slot_of = [wrap, 1 - wrap]
    w_to = []
    for blk in range(2):
        for yt in (hb, 3 - hb):
            w_to.append((blk, yt, (1 - xbit) * c + xbit * blk))
    w_from = [dev(half, c, z, x)] * 2 + [dev(2, half, z, x), dev(3, half, z, x)]
    flip = dev(y, c, z, x)

    barrier = pltpu.get_barrier_semaphore()
    partners = [sib, mate, diag, twin, flip]
    partners += [dev(y, cc, z, yt) for _, yt, cc in w_to] + w_from
    partners += [dev(up_x, c, z, y), dev(dn_x, c, z, y), dev(x, c, up_z, y), dev(x, c, dn_z, y)]
    partners += halo_to + halo_from
    for to in partners:
        pl.semaphore_signal(barrier, inc=1, device_id=to, device_id_type=pl.DeviceIdType.MESH)
    pl.semaphore_wait(barrier, len(partners))

    pending = []

    def go(copy):
        copy.start()
        pending.append(copy)
        return copy

    features = pl.ds(pl.multiple_of(640 * x, 128), 640)
    dsrc = d_ref.at[pl.ds(pl.multiple_of(96 * c, 32), 96), features]
    ddst = dn.at[z, pl.ds(pl.multiple_of(96 * g, 32), 96), features]
    dloc = pltpu.make_async_copy(dsrc, ddst, d_sem.at[0])
    dloc.start()
    dsend = go(remote(dsrc, ddst, d_send.at[0], d_sem.at[1], twin))

    w_copies = []
    for n, (blk, yt, cc) in enumerate(w_to):
        src = w_ref.at[:, blk * 256 : (blk + 1) * 256]
        cb = (1 - xbit) * blk + xbit * x
        dst = wb.at[cb, z, y]
        here = (y == x) & (yt == y) & (cc == c)
        copy = remote(src, dst, w_send.at[n], w_sem.at[cb], dev(y, cc, z, yt))
        w_copies.append((here, copy))

        @pl.when(here)
        def _():
            pltpu.make_async_copy(src, dst, w_sem.at[cb]).start()

        @pl.when(jnp.logical_not(here))
        def _():
            copy.start()

    u_copies = []
    kvx = c + 2 * half_of(x)
    for cb in (2, 3, 0, 1):
        col = kvx * 512 + cb * 256 if cb < 2 else cb * 1024 + kvx * 256
        src = u_ref.at[:, pl.ds(pl.multiple_of(col, 128), 256)]
        dst = ub.at[cb, z, y]
        copy = remote(src, dst, u_send.at[cb], u_sem.at[cb], flip)
        u_copies.append(copy)

        @pl.when(x == y)
        def _():
            pltpu.make_async_copy(src, dst, u_sem.at[cb]).start()

        @pl.when(x != y)
        def _():
            copy.start()

    own = 2 * c + yl
    pltpu.make_async_copy(ids_ref, ids.at[own], i_recv.at[own]).start()
    for k, to in enumerate((sib, mate, diag)):
        go(remote(ids_ref, ids.at[own], i_send.at[k], i_recv.at[own], to))

    def block_rows(blk, k):
        return xg.at[pl.ds(pl.multiple_of(blk * 512 + k * 128, 128), 128), :]

    def to_mate(k):
        ref = block_rows(own, k)
        return remote(ref, ref, x_send.at[0, k], x_recv.at[0, k], mate)

    def forward(k):
        ref = block_rows(2 * c + 1 - yl, k)
        return remote(ref, ref, f_send.at[k], x_recv.at[2, k], sib)

    for k in range(4):
        val = x_ref[k * 128 : (k + 1) * 128, :].astype(F32)
        scale = lax.rsqrt(jnp.mean(val * val, axis=-1, keepdims=True) + 1e-06)
        ref = block_rows(own, k)
        ref[...] = (val * scale * g_ref[...]).astype(BF16)

        @pl.when(c == 0)
        def _():
            to_mate(k).start()

        go(remote(ref, ref, x_send.at[1, k], x_recv.at[1, k], sib))

    def slots(cls, part, stage, i, h):
        out = []
        if cls == 0:
            rows = pl.ds(part * 96, 96) if h is None else pl.ds(part * 96 + h * 48, 48)
            cols_i = pl.ds(pl.multiple_of(i * 640, 128), 640)
            if part == 0:
                out.append(dn.at[z, rows, cols_i] if stage == 0 else dn.at[i, rows, :])
            else:
                out.append(dn.at[i, rows, features] if stage == 0 else dn.at[:, rows, cols_i])
            return out
        cb = (2, 0)[cls - 1] + part
        for buf, size in ((wb, 160), (ub, 64)):
            rows = pl.ds(0, size) if h is None else pl.ds(h * (size // 2), size // 2)
            if part == 0:
                out.append(buf.at[cb, z, i, rows, :] if stage == 0 else buf.at[cb, i, :, rows, :])
            else:
                out.append(buf.at[cb, i, x, rows, :] if stage == 0 else buf.at[cb, :, i, rows, :])
        return out

    def step(cls, s):
        copies = []
        stage = s // 2
        for part in range(2):
            along_x = (part == 0) == (stage == 0)
            me, up, dw = (x, up_x, dn_x) if along_x else (z, up_z, dn_z)
            to_up = dev(up, c, z, y) if along_x else dev(x, c, up, y)
            to_dn = dev(dw, c, z, y) if along_x else dev(x, c, dw, y)
            for way, to in enumerate((to_up, to_dn)):
                if s % 2 == 0:
                    refs = slots(cls, part, stage, me, None)
                else:
                    refs = slots(cls, part, stage, dw if way == 0 else up, way)
                for n, ref in enumerate(refs):
                    at = (2 * cls + part, s, 2 * way + n)
                    copies.append(go(remote(ref, ref, g_send.at[at], g_recv.at[at], to)))
        return copies

    def done(copies):
        for copy in copies:
            copy.wait_recv()

    dloc.wait()
    dsend.wait_recv()
    dd = step(0, 0)
    for cb in (2, 3):
        arrived(wb.at[cb, z, x], w_sem.at[cb])
        arrived(ub.at[cb, z, x], u_sem.at[cb])
    kk = step(1, 0)
    done(dd)
    dd = step(0, 1)
    for cb in (0, 1):
        arrived(wb.at[cb, z, x], w_sem.at[cb])
        arrived(ub.at[cb, z, x], u_sem.at[cb])
    qq = step(2, 0)
    done(dd)
    dd = step(0, 2)
    done(kk)
    kk = step(1, 1)
    done(qq)
    qq = step(2, 1)

    for k in range(4):
        arrived(ids.at[k], i_recv.at[k])
    for blk in range(4):
        for k in range(4):
            at = slice(blk * 512 + k * 128, blk * 512 + (k + 1) * 128)
            acol[at, :] = jnp.broadcast_to(ids[blk, k : k + 1, :], (128, 128)).T
            scol[at, :] = jnp.broadcast_to(ids[blk, 4 + k : 5 + k, :], (128, 128)).T
    for r in range(2):
        ref = ids.at[2 * r : 2 * r + 2]
        go(remote(ref, hids.at[slot_of[r]], h_send.at[8 + r], h_recv.at[slot_of[r], 4], halo_to[r]))
    for k in range(4):
        arrived(block_rows(0, 0), x_recv.at[1, k])

    done(kk)
    done(dd)
    dd = step(0, 3)
    kk = step(1, 2)

    @pl.when(c == 0)
    def _():
        for k in range(4):
            arrived(block_rows(0, 0), x_recv.at[0, k])
            forward(k).start()

    @pl.when(c == 1)
    def _():
        for k in range(4):
            arrived(block_rows(0, 0), x_recv.at[2, k])
            to_mate(k).start()

    done(dd)

    def ranks(blk, carry):
        rows = pl.ds(pl.multiple_of(blk * 512, 512), 512)
        vals = jnp.concatenate(
            [dot(xg[rows, :], dn[k], ((1,), (1,))).astype(BF16) for k in range(4)], axis=1
        )
        first = (c * 2 + half * 4).astype(F32)
        apart = (12 - 8 * half).astype(F32)
        mine = acol[rows, 0:1] == cols_ref[0:1, :] + cols_ref[1:2, :] * apart + first
        kept_vals = jnp.where(mine, vals.astype(F32), 0.0).astype(BF16)
        rpt[own, :, rows] = dot(fold_ref[...], kept_vals, ((1,), (1,))).astype(BF16)
        for k, to in enumerate((sib, mate, diag)):
            ref = rpt.at[own, :, rows]
            remote(ref, ref, r_send.at[k, blk], r_recv.at[own, blk], to).start()
        return carry

    lax.fori_loop(0, 2, ranks, 0)
    done(qq)
    done(kk)
    kk = step(1, 3)
    qq = step(2, 2)

    lane = lax.broadcasted_iota(jnp.int32, (1, 128), 1)
    lane_adapter = (lane // 16).astype(F32)

    def halo_copies(blk):
        r, part = blk // 2, blk % 2
        src = pl.ds(pl.multiple_of(1024 + part * 512, 512), 512)
        dst = pl.ds(pl.multiple_of(part * 512, 512), 512)
        sl = (r + wrap) % 2
        to = dev((x + wrap * r) % 4, c, tz, y3)
        return [
            remote(buf.at[r, src, :], buf.at[sl, dst, :], h_send.at[2 * blk + n],
                   h_recv.at[sl, part * 2 + n], to)
            for n, buf in enumerate((kall, vall))
        ]

    def project(blk, kinds):
        rows = pl.ds(pl.multiple_of(blk * 512, 512), 512)
        total_ranks = rpt[0, :, rows].astype(F32)
        for k in range(1, 4):
            total_ranks = total_ranks + rpt[k, :, rows].astype(F32)
        tiled = dot(total_ranks.T.astype(BF16), tile_ref[...])
        adapters = acol[rows, :]
        for part, col_blocks in kinds:
            mine = tiled[:, part * 128 : (part + 1) * 128]
            spread = jnp.concatenate(
                [
                    jnp.where(adapters == lane_adapter + 8.0 * n, mine, 0.0).astype(BF16)
                    for n in range(8)
                ],
                axis=1,
            )
            for cb in col_blocks:
                base = dot(xg[rows, :], wb[cb].reshape(WIDTH, 256))
                delta = dot(spread, ub[cb].reshape(1024, 256))
                proj = base.astype(BF16).astype(F32) + delta.astype(BF16).astype(F32)
                if cb < 3:
                    scale = lax.rsqrt(jnp.mean(proj * proj, axis=-1, keepdims=True) + 1e-06)
                    gain = gains_ref[0:1, :] if cb < 2 else gains_ref[1:2, :]
                    proj = proj * scale * gain
                val = proj.astype(BF16)
                at = pl.ds(pl.multiple_of(1024 + (blk % 2) * 512, 512), 512)
                if cb < 2:
                    qs[cb, rows, :] = val * BF16(0.0625)
                elif cb == 2:
                    kall[blk // 2, at, :] = val
                else:
                    vall[blk // 2, at, :] = val

    def project_kv(n, carry):
        blk = n // 2 * 2 + 1 - n % 2
        for k in range(1, 4):
            src = (own + k) % 4
            arrived(rpt.at[src, :, pl.ds(0, 512)], r_recv.at[src, blk])
        project(blk, ((1, (2,)), (2, (3,))))
        for copy in halo_copies(blk):
            copy.start()
        return carry

    def project_q(blk, carry):
        project(blk, ((0, (0, 1)),))
        return carry

    done(kk)
    lax.fori_loop(0, 2, project_kv, 0)
    done(qq)
    qq = step(2, 3)

    @pl.when(c == 1)
    def _():
        for k in range(4):
            arrived(block_rows(0, 0), x_recv.at[0, k])
            forward(k).start()

    @pl.when(c == 0)
    def _():
        for k in range(4):
            arrived(block_rows(0, 0), x_recv.at[2, k])

    lax.fori_loop(2, 4, ranks, 0)
    done(qq)
    lax.fori_loop(0, 2, project_q, 0)
    lax.fori_loop(2, 4, project_kv, 0)
    lax.fori_loop(2, 4, project_q, 0)

    for sl in range(2):
        arrived(hids.at[sl], h_recv.at[sl, 4])
    nothing = jnp.where(x * 8 + z * 2 + g == 0, 1.0, 0.0).astype(F32)
    for r in range(2):
        for t in range(8):
            blk, k = (t % 4) // 2, (t % 2) * 2
            if t < 4:
                pair = [hids[r, blk, 4 + k + n : 5 + k + n, :] for n in range(2)]
                if r == 0:
                    pair = [p - nothing * (p + 1.0) for p in pair]
            else:
                pair = [ids[2 * r + blk, 4 + k + n : 5 + k + n, :] for n in range(2)]
            krow[r, t] = jnp.broadcast_to(jnp.concatenate(pair, axis=1), (8, 256))

    ahead = lax.broadcasted_iota(jnp.int32, (256, 256), 0) - lax.broadcasted_iota(
        jnp.int32, (256, 256), 1
    )

    def attend(r, i, h, tiles, acc, total):
        rows = slice(r * 1024 + i * 256, r * 1024 + (i + 1) * 256)
        q = qs[h, rows, :]
        sq = scol[rows, 0:1]
        for t in tiles:
            keys = slice(t * 256, (t + 1) * 256)
            s = dot(q, kall[r, keys, :], ((1,), (1,)))
            ok = sq == krow[r, t, 0:1, :]
            if t == i:
                ok = ok & (ahead < 0)
            if t == i + 4:
                ok = ok & (ahead >= 0)
            w = jnp.where(ok, jnp.exp(s), 0.0)
            more = w[:, 0:128] + w[:, 128:256]
            part = dot(w.astype(BF16), vall[r, keys, :])
            total = more if total is None else total + more
            acc = part if acc is None else acc + part
        return acc, total

    def attend_own(r):
        for i in range(4):
            at = slice(i * 256, (i + 1) * 256)

            def head(h, carry):
                acc, total = attend(r, i, h, range(4, 5 + i), None, None)
                acc_ref[h, at, :] = acc
                tot_ref[h, at, :] = total
                return carry

            lax.fori_loop(0, 2, head, 0)

    def out_copy(blk):
        src = ob.at[:, blk * 512 : (blk + 1) * 512, :]
        refs = []
        for h in range(2):
            dst = out_ref.at[:, pl.ds(pl.multiple_of(kv * 512 + h * 256, 256), 256)]
            refs.append((src.at[h], dst))
        return refs, dev(x, blk // 2, z, g * 2 + blk % 2)

    def attend_halo(r, part):
        for i in (2 * part + 1, 2 * part):
            at = slice(i * 256, (i + 1) * 256)
            rows = slice(r * 1024 + i * 256, r * 1024 + (i + 1) * 256)

            def head(h, carry):
                acc, total = attend(r, i, h, range(i, 4), acc_ref[h, at, :], tot_ref[h, at, :])
                norm = jnp.sum(total, axis=-1, keepdims=True)
                ob[h, rows, :] = (acc / norm).astype(BF16)
                return carry

            lax.fori_loop(0, 2, head, 0)
        blk = 2 * r + part
        refs, to = out_copy(blk)

        @pl.when(blk == own)
        def _():
            for h, (src, dst) in enumerate(refs):
                pltpu.make_async_copy(src, dst, o_recv.at[own, h]).start()

        @pl.when(blk != own)
        def _():
            for h, (src, dst) in enumerate(refs):
                remote(src, dst, o_send.at[blk, h], o_recv.at[own, h], to).start()

    for r in range(2):
        attend_own(r)
        for part in (1, 0):
            for n in range(2):
                arrived(kall.at[r, pl.ds(0, 512), :], h_recv.at[r, 2 * part + n])
            attend_halo(r, part)

    for k in range(4):
        for h in range(2):
            arrived(out_ref.at[:, pl.ds(0, 256)], o_recv.at[k, h])
    for blk in range(4):
        refs, to = out_copy(blk)

        @pl.when(blk != own)
        def _():
            for h, (src, dst) in enumerate(refs):
                remote(src, dst, o_send.at[blk, h], o_recv.at[own, h], to).wait_send()

        for k, to in enumerate((sib, mate, diag)):
            ref = rpt.at[own, :, pl.ds(0, 512)]
            remote(ref, ref, r_send.at[k, blk], r_recv.at[own, blk], to).wait_send()
        for copy in halo_copies(blk):
            copy.wait_send()
    for k in range(4):
        to_mate(k).wait_send()
        forward(k).wait_send()
    for here, copy in w_copies:

        @pl.when(jnp.logical_not(here))
        def _():
            copy.wait_send()

    for copy in u_copies:

        @pl.when(x != y)
        def _():
            copy.wait_send()

    for copy in pending:
        copy.wait_send()


FOLD = np.zeros((48, 768), np.float32)
FOLD[np.arange(768) % 48, np.arange(768)] = 1.0
TILE = np.zeros((48, 384), np.float32)
for _lane in range(384):
    TILE[(_lane // 128) * 16 + _lane % 16, _lane] = 1.0
_c = np.arange(768)
COLS = np.zeros((8, 768), np.float32)
COLS[0] = (_c // 192) * 16 + _c % 96 // 48
COLS[1] = _c % 192 // 96


def body(
    residual_input,
    input_norm_gain,
    base_projection_weight,
    query_key_gains,
    adapter_down_weight,
    adapter_up_weight,
    row_adapter_index,
    row_sequence_index,
):
    ids = jnp.concatenate(
        [row_adapter_index.reshape(4, 128), row_sequence_index.reshape(4, 128)], axis=0
    ).astype(F32)
    down = jnp.transpose(adapter_down_weight, (0, 2, 1)).reshape(192, WIDTH)
    up = adapter_up_weight.reshape(64, 4096)
    vm = pl.BlockSpec(memory_space=pltpu.VMEM)
    anyspace = pl.BlockSpec(memory_space=pl.ANY)
    dma = pltpu.SemaphoreType.DMA
    return pl.pallas_call(
        kernel,
        out_shape=jax.ShapeDtypeStruct((ROWS, HEADS * HEAD_DIM), BF16),
        in_specs=[vm] * 7 + [anyspace] * 3,
        out_specs=anyspace,
        scratch_shapes=[
            pltpu.VMEM((2048, WIDTH), BF16),
            pltpu.VMEM((4, 4, 4, 160, 256), BF16),
            pltpu.VMEM((4, 4, 4, 64, 256), BF16),
            pltpu.VMEM((4, 192, WIDTH), BF16),
            pltpu.VMEM((4, 48, 2048), BF16),
            pltpu.VMEM((2, 2048, 256), BF16),
            pltpu.VMEM((2, 2048, 256), BF16),
            pltpu.VMEM((2, 2048, 256), BF16),
            pltpu.VMEM((2, 2048, 256), BF16),
            pltpu.VMEM((2, 1024, 256), F32),
            pltpu.VMEM((2, 1024, 128), F32),
            pltpu.VMEM((4, 8, 128), F32),
            pltpu.VMEM((2, 2, 8, 128), F32),
            pltpu.VMEM((2048, 128), F32),
            pltpu.VMEM((2048, 128), F32),
            pltpu.VMEM((2, 8, 8, 256), F32),
            dma((1,)), dma((2,)), dma((4,)), dma((4,)), dma((4,)), dma((4,)),
            dma((2, 4)), dma((3, 4)), dma((4,)),
            dma((3,)), dma((4,)),
            dma((6, 4, 4)), dma((6, 4, 4)),
            dma((3, 4)), dma((4, 4)),
            dma((10,)), dma((2, 5)),
            dma((4, 2)), dma((4, 2)),
        ],
        compiler_params=pltpu.CompilerParams(
            collective_id=0, has_side_effects=True, vmem_limit_bytes=60 << 20
        ),
        name="block",
    )(
        residual_input,
        input_norm_gain.reshape(1, WIDTH),
        query_key_gains,
        ids,
        jnp.asarray(FOLD, BF16),
        jnp.asarray(TILE, BF16),
        jnp.asarray(COLS),
        base_projection_weight,
        down,
        up,
    )


def solution(mesh):
    placed = (
        P(("dp", "adapter"), None),
        P(),
        P("adapter", "dp"),
        P(),
        P("adapter", None, None),
        P("adapter", None, None),
        P(("dp", "adapter"), None),
        P(("dp", "adapter")),
    )
    return jax.shard_map(
        body, mesh=mesh, in_specs=placed, out_specs=P(("dp", "adapter"), None), check_vma=False
    )
```

```python
import jax
import jax.numpy as jnp
import numpy as np
from jax import lax
from jax.experimental import pallas as pl
from jax.experimental.pallas import tpu as pltpu
from jax.sharding import PartitionSpec as P

HEADS = 8
KV_HEADS = 4
HEAD_DIM = 256
ROWS = 512
WIDTH = 2560
BF16 = jnp.bfloat16
F32 = jnp.float32


def dot(a, b, dims=((1,), (0,))):
    return lax.dot_general(a, b, (dims, ((), ())), preferred_element_type=F32)


def kernel(
    x_ref, g_ref, gains_ref, aid_ref, sid_ref, fold_ref, tile_ref, cols_ref, w_ref, d_ref, u_ref,
    out_ref,
    xg, wu, dn, rpt, qs, kall, vall, ob, acc_ref, tot_ref, ids, hids, acol, scol, krow,
    sh_send, d_sem, u_sem, w_sem, x_send, x_recv, f_send, i_send, i_recv,
    g_send, g_recv, r_send, r_recv, h_send, h_recv, o_send, o_recv,
):
    dp = lax.axis_index("dp")
    ad = lax.axis_index("adapter")
    x, c = dp // 2, dp % 2
    z, y = ad // 4, ad % 4
    g, yl = y // 2, y % 2

    def dev(x_, c_, z_, y_):
        return (x_ * 2 + c_, z_ * 4 + y_)

    def half_of(y_):
        return ((y_ + 1) // 2) % 2

    def remote(src, dst, ssem, rsem, to):
        return pltpu.make_async_remote_copy(
            src_ref=src, dst_ref=dst, send_sem=ssem, recv_sem=rsem,
            device_id=to, device_id_type=pl.DeviceIdType.MESH,
        )

    def arrived(ref, sem):
        pltpu.make_async_copy(ref, ref, sem).wait()

    half = half_of(y)
    kv = c + 2 * half
    ypar = 1 - 2 * yl + y
    sib = dev(x, 1 - c, z, y)
    mate = dev(x, c, z, ypar)
    diag = dev(x, 1 - c, z, ypar)
    xbit = x // 2
    b = (1 - xbit) * (x % 2) + xbit * c
    px = (1 - xbit) * (1 - x) + xbit * x
    pc = (1 - xbit) * c + xbit * (1 - c)
    up_x, dn_x = (x + 1) % 4, (x + 3) % 4
    up_z, dn_z = (z + 1) % 4, (z + 3) % 4
    y3 = 3 - y
    wrap = g * (z // 3)
    tz = (z + g) % 4
    swrap = (1 - g) * ((3 - z) // 3)
    sz = (z + 3 + g) % 4
    halo_to = [dev(x, c, tz, y3), dev((x + wrap) % 4, c, tz, y3)]
    halo_from = [dev((x + 4 - swrap) % 4, c, sz, y3), dev(x, c, sz, y3)]
    slot_of = [wrap, 1 - wrap]

    barrier = pltpu.get_barrier_semaphore()
    partners = [sib, mate, diag]
    partners += [dev(x, c, z, (y + k) % 4) for k in (1, 2, 3)]
    partners += [dev(px, pc, z, k) for k in range(4)]
    partners += [dev(up_x, c, z, y), dev(dn_x, c, z, y), dev(x, c, up_z, y), dev(x, c, dn_z, y)]
    partners += halo_to + halo_from
    for to in partners:
        pl.semaphore_signal(barrier, inc=1, device_id=to, device_id_type=pl.DeviceIdType.MESH)
    pl.semaphore_wait(barrier, len(partners))

    pending = []

    def go(copy):
        copy.start()
        pending.append(copy)
        return copy

    y2 = (y + 2) % 4
    dsrc = d_ref.at[pl.ds(pl.multiple_of(96 * c, 32), 96), pl.ds(pl.multiple_of(640 * x, 128), 640)]
    ddst = dn.at[z, pl.ds(pl.multiple_of(96 * g, 32), 96), pl.ds(pl.multiple_of(640 * x, 128), 640)]
    dloc = pltpu.make_async_copy(dsrc, ddst, d_sem.at[0])
    dloc.start()
    dsend = go(remote(dsrc, ddst, sh_send.at[0], d_sem.at[1], dev(x, c, z, y2)))

    def up_src(y_):
        kv_ = c + 2 * half_of(y_)
        col = (1 - xbit) * (kv_ * 512 + x * 256) + xbit * (2048 + (x - 2) * 1024 + kv_ * 256)
        return u_ref.at[:, pl.ds(pl.multiple_of(col, 128), 256)]

    udst = wu.at[x, z, pl.ds(pl.multiple_of(640 + 64 * y, 64), 64), :]
    for k in (1, 2, 3):
        yt = (y + k) % 4
        go(remote(up_src(yt), udst, sh_send.at[k], u_sem.at[y], dev(x, c, z, yt)))
    pltpu.make_async_copy(up_src(y), udst, u_sem.at[y]).start()
    kept = w_ref.at[:, pl.ds(pl.multiple_of(b * 256, 256), 256)]
    other = w_ref.at[:, pl.ds(pl.multiple_of((1 - b) * 256, 256), 256)]
    wrows = pl.ds(pl.multiple_of(160 * y, 32), 160)
    kept_sends = []
    for k, yt in enumerate((b, 3 - b)):
        send = remote(kept, wu.at[x, z, wrows, :], sh_send.at[4 + k], w_sem.at[y], dev(x, c, z, yt))
        kept_sends.append((yt, send))

        @pl.when(yt == y)
        def _():
            pltpu.make_async_copy(kept, wu.at[x, z, wrows, :], w_sem.at[y]).start()

        @pl.when(yt != y)
        def _():
            send.start()

        go(remote(other, wu.at[px, z, wrows, :], sh_send.at[6 + k], w_sem.at[y], dev(px, pc, z, yt)))

    own = 2 * c + yl
    ids[own] = jnp.concatenate([aid_ref[...], sid_ref[...]], axis=0).astype(F32)
    for k in range(4):
        val = x_ref[k * 128 : (k + 1) * 128, :].astype(F32)
        scale = lax.rsqrt(jnp.mean(val * val, axis=-1, keepdims=True) + 1e-06)
        rows = pl.ds(pl.multiple_of(own * 512 + k * 128, 128), 128)
        xg[rows, :] = (val * scale * g_ref[...].reshape(1, WIDTH)).astype(BF16)
        go(remote(xg.at[rows, :], xg.at[rows, :], x_send.at[1, k], x_recv.at[1, k], sib))

    for k, to in enumerate((sib, mate, diag)):
        go(remote(ids.at[own], ids.at[own], i_send.at[k], i_recv.at[own], to))

    def block_rows(blk, k):
        return xg.at[pl.ds(pl.multiple_of(blk * 512 + k * 128, 128), 128), :]

    def slot(part, stage, i, lo, n):
        if part < 2:
            rows = pl.ds(part * 96 + lo, n)
            cols_i = pl.ds(pl.multiple_of(i * 640, 128), 640)
            cols_x = pl.ds(pl.multiple_of(x * 640, 128), 640)
            if part == 0:
                return dn.at[z, rows, cols_i] if stage == 0 else dn.at[i, rows, :]
            return dn.at[i, rows, cols_x] if stage == 0 else dn.at[:, rows, cols_i]
        rows = pl.ds((part - 2) * 448 + lo, n)
        if part == 2:
            return wu.at[i, z, rows, :] if stage == 0 else wu.at[:, i, rows, :]
        return wu.at[x, i, rows, :] if stage == 0 else wu.at[i, :, rows, :]

    def step(part, s):
        size = 96 if part < 2 else 448
        stage = s // 2
        along_x = (part % 2 == 0) == (stage == 0)
        me, up, dw = (x, up_x, dn_x) if along_x else (z, up_z, dn_z)
        to_up = dev(up, c, z, y) if along_x else dev(x, c, up, y)
        to_dn = dev(dw, c, z, y) if along_x else dev(x, c, dw, y)
        copies = []
        for way, to in enumerate((to_up, to_dn)):
            if s % 2 == 0:
                ref = slot(part, stage, me, 0, size)
            else:
                ref = slot(part, stage, dw if way == 0 else up, way * (size // 2), size // 2)
            copies.append(
                go(remote(ref, ref, g_send.at[part, s, way], g_recv.at[part, s, way], to))
            )
        return copies

    def done(copies):
        for copy in copies:
            copy.wait_recv()

    dloc.wait()
    dsend.wait_recv()
    d1, d2 = step(0, 0), step(1, 0)
    for k in range(4):
        arrived(wu.at[x, z, pl.ds(640 + 64 * k, 64), :], u_sem.at[k])
        arrived(wu.at[x, z, pl.ds(160 * k, 160), :], w_sem.at[k])
    w1, w2 = step(2, 0), step(3, 0)
    for k in range(4):
        ref = block_rows(own, k)
        go(remote(ref, ref, x_send.at[0, k], x_recv.at[0, k], mate))
    done(d1), done(d2)
    d1, d2 = step(0, 1), step(1, 1)
    done(d1), done(d2)
    d1, d2 = step(0, 2), step(1, 2)
    done(w1), done(w2)
    w1, w2 = step(2, 1), step(3, 1)
    done(d1), done(d2)
    d1, d2 = step(0, 3), step(1, 3)
    done(w1), done(w2)
    w1, w2 = step(2, 2), step(3, 2)

    for k in range(1, 4):
        arrived(ids.at[0], i_recv.at[(own + k) % 4])
    for blk in range(4):
        for k in range(4):
            at = slice(blk * 512 + k * 128, blk * 512 + (k + 1) * 128)
            acol[at, :] = jnp.broadcast_to(ids[blk, k : k + 1, :], (128, 128)).T
            scol[at, :] = jnp.broadcast_to(ids[blk, 4 + k : 5 + k, :], (128, 128)).T
    for r in range(2):
        ref = ids.at[2 * r : 2 * r + 2]
        go(remote(ref, hids.at[slot_of[r]], h_send.at[8 + r], h_recv.at[slot_of[r], 4], halo_to[r]))
    for k in range(4):
        arrived(block_rows(0, 0), x_recv.at[1, k])

    done(d1), done(d2)

    def ranks(o):
        blk = ((c + o) % 2) * 2 + (yl + o // 2) % 2
        rows = pl.ds(pl.multiple_of(blk * 512, 512), 512)
        vals = jnp.concatenate(
            [dot(xg[rows, :], dn[k], ((1,), (1,))).astype(BF16) for k in range(4)], axis=1
        )
        first = (c * 2 + yl * 4).astype(F32)
        mine = acol[rows, 0:1] == cols_ref[0:1, :] + first
        kept_vals = jnp.where(mine, vals.astype(F32), 0.0).astype(BF16)
        rpt[own, :, rows] = dot(fold_ref[...], kept_vals, ((1,), (1,))).astype(BF16)
        for k, to in enumerate((sib, mate, diag)):
            ref = rpt.at[own, :, rows]
            remote(ref, ref, r_send.at[k, o], r_recv.at[own, blk], to).start()

    def two_ranks(first):
        def run(o, carry):
            ranks(o)
            return carry

        lax.fori_loop(first, first + 2, run, 0)

    two_ranks(0)
    done(w1), done(w2)
    w1, w2 = step(2, 3), step(3, 3)
    forwards = []
    mblk = 2 * c + 1 - yl
    for k in range(4):
        arrived(block_rows(0, 0), x_recv.at[0, k])
        ref = block_rows(mblk, k)
        forwards.append(go(remote(ref, ref, f_send.at[k], x_recv.at[2, k], sib)))
    done(forwards)
    two_ranks(2)
    done(w1), done(w2)

    lane = lax.broadcasted_iota(jnp.int32, (1, 128), 1)
    lane_adapter = (lane // 16).astype(F32)

    def halo_copies(blk, o):
        r, part = blk // 2, blk % 2
        src = pl.ds(pl.multiple_of(1024 + part * 512, 512), 512)
        dst = pl.ds(pl.multiple_of(part * 512, 512), 512)
        sl = (r + wrap) % 2
        to = dev((x + wrap * r) % 4, c, tz, y3)
        return [
            remote(buf.at[r, src, :], buf.at[sl, dst, :], h_send.at[2 * o + n],
                   h_recv.at[sl, part * 2 + n], to)
            for n, buf in enumerate((kall, vall))
        ]

    def project(blk, kinds):
        rows = pl.ds(pl.multiple_of(blk * 512, 512), 512)
        total_ranks = rpt[0, :, rows].astype(F32)
        for k in range(1, 4):
            total_ranks = total_ranks + rpt[k, :, rows].astype(F32)
        tiled = dot(total_ranks.T.astype(BF16), tile_ref[...])
        adapters = acol[rows, :]
        for part, col_blocks in kinds:
            mine = tiled[:, part * 128 : (part + 1) * 128]
            spread = [
                jnp.where(adapters == lane_adapter + 8.0 * n, mine, 0.0).astype(BF16)
                for n in range(8)
            ]
            for cb in col_blocks:
                base = jnp.zeros((512, 256), F32)
                delta = jnp.zeros((512, 256), F32)
                for k in range(4):
                    base = base + dot(xg[rows, k * 640 : (k + 1) * 640], wu[cb, k, 0:640, :])
                    pair = jnp.concatenate([spread[2 * k], spread[2 * k + 1]], axis=1)
                    delta = delta + dot(pair, wu[cb, k, 640:896, :])
                proj = base.astype(BF16).astype(F32) + delta.astype(BF16).astype(F32)
                if cb < 3:
                    scale = lax.rsqrt(jnp.mean(proj * proj, axis=-1, keepdims=True) + 1e-06)
                    gain = gains_ref[0:1, :] if cb < 2 else gains_ref[1:2, :]
                    proj = proj * scale * gain
                val = proj.astype(BF16)
                at = pl.ds(pl.multiple_of(1024 + (blk % 2) * 512, 512), 512)
                if cb < 2:
                    qs[cb, rows, :] = val * BF16(0.0625)
                elif cb == 2:
                    kall[blk // 2, at, :] = val
                else:
                    vall[blk // 2, at, :] = val

    def project_kv(o, carry):
        blk = o // 2 * 2 + 1 - o % 2
        for k in range(1, 4):
            src = (own + k) % 4
            arrived(rpt.at[src, :, pl.ds(0, 512)], r_recv.at[src, blk])
        project(blk, ((1, (2,)), (2, (3,))))
        for copy in halo_copies(blk, o):
            copy.start()
        return carry

    def project_q(blk, carry):
        project(blk, ((0, (0, 1)),))
        return carry

    lax.fori_loop(0, 4, project_kv, 0)
    lax.fori_loop(0, 4, project_q, 0)

    for sl in range(2):
        arrived(hids.at[sl], h_recv.at[sl, 4])
    nothing = jnp.where(x * 8 + z * 2 + g == 0, 1.0, 0.0).astype(F32)
    for r in range(2):
        for t in range(8):
            blk, k = (t % 4) // 2, (t % 2) * 2
            if t < 4:
                pair = [hids[r, blk, 4 + k + n : 5 + k + n, :] for n in range(2)]
                if r == 0:
                    pair = [p - nothing * (p + 1.0) for p in pair]
            else:
                pair = [ids[2 * r + blk, 4 + k + n : 5 + k + n, :] for n in range(2)]
            krow[r, t] = jnp.broadcast_to(jnp.concatenate(pair, axis=1), (8, 256))

    ahead = lax.broadcasted_iota(jnp.int32, (256, 256), 0) - lax.broadcasted_iota(
        jnp.int32, (256, 256), 1
    )

    def attend(r, i, h, tiles, acc, total):
        rows = slice(r * 1024 + i * 256, r * 1024 + (i + 1) * 256)
        q = qs[h, rows, :]
        sq = scol[rows, 0:1]
        for t in tiles:
            keys = slice(t * 256, (t + 1) * 256)
            s = dot(q, kall[r, keys, :], ((1,), (1,)))
            ok = sq == krow[r, t, 0:1, :]
            if t == i:
                ok = ok & (ahead < 0)
            if t == i + 4:
                ok = ok & (ahead >= 0)
            w = jnp.where(ok, jnp.exp(s), 0.0)
            more = w[:, 0:128] + w[:, 128:256]
            part = dot(w.astype(BF16), vall[r, keys, :])
            total = more if total is None else total + more
            acc = part if acc is None else acc + part
        return acc, total

    def attend_own(r):
        for i in range(4):
            at = slice(i * 256, (i + 1) * 256)

            def head(h, carry):
                acc, total = attend(r, i, h, range(4, 5 + i), None, None)
                acc_ref[h, at, :] = acc
                tot_ref[h, at, :] = total
                return carry

            lax.fori_loop(0, 2, head, 0)

    def out_copy(blk, m):
        src = ob.at[pl.ds(blk * 512 + m * 256, 256), :]
        dst = out_ref.at[m * 256 : (m + 1) * 256, pl.ds(pl.multiple_of(kv * 512, 512), 512)]
        return src, dst, dev(x, blk // 2, z, g * 2 + blk % 2)

    def attend_halo(r, part):
        for i in (2 * part + 1, 2 * part):
            at = slice(i * 256, (i + 1) * 256)
            rows = slice(r * 1024 + i * 256, r * 1024 + (i + 1) * 256)

            def head(h, carry):
                acc, total = attend(r, i, h, range(i, 4), acc_ref[h, at, :], tot_ref[h, at, :])
                norm = jnp.sum(total, axis=-1, keepdims=True)
                ob[rows, pl.ds(pl.multiple_of(h * 256, 256), 256)] = (acc / norm).astype(BF16)
                return carry

            lax.fori_loop(0, 2, head, 0)
            blk, m = 2 * r + part, i % 2
            src, dst, to = out_copy(blk, m)

            @pl.when(blk == own)
            def _():
                pltpu.make_async_copy(src, dst, o_recv.at[own, m]).start()

            @pl.when(blk != own)
            def _():
                remote(src, dst, o_send.at[blk, m], o_recv.at[own, m], to).start()

    for r in range(2):
        attend_own(r)
        for part in (1, 0):
            for n in range(2):
                arrived(kall.at[r, pl.ds(0, 512), :], h_recv.at[r, 2 * part + n])
            attend_halo(r, part)

    for k in range(4):
        for m in range(2):
            arrived(out_ref.at[0:256, pl.ds(0, 512)], o_recv.at[k, m])
    for blk in range(4):

        @pl.when(blk != own)
        def _():
            for m in range(2):
                src, dst, to = out_copy(blk, m)
                remote(src, dst, o_send.at[blk, m], o_recv.at[own, m], to).wait_send()

    for o in range(4):
        for k, to in enumerate((sib, mate, diag)):
            ref = rpt.at[own, :, pl.ds(0, 512)]
            remote(ref, ref, r_send.at[k, o], r_recv.at[own, o], to).wait_send()
        blk = o // 2 * 2 + 1 - o % 2
        for copy in halo_copies(blk, o):
            copy.wait_send()
    for yt, send in kept_sends:

        @pl.when(yt != y)
        def _():
            send.wait_send()

    for copy in pending:
        copy.wait_send()


FOLD = np.zeros((48, 768), np.float32)
FOLD[np.arange(768) % 48, np.arange(768)] = 1.0
TILE = np.zeros((48, 384), np.float32)
for _lane in range(384):
    TILE[(_lane // 128) * 16 + _lane % 16, _lane] = 1.0
_c = np.arange(768)
COLS = np.tile(((_c // 192) * 16 + (_c % 192 // 96) * 8 + _c % 96 // 48).astype(np.float32), (8, 1))


def body(
    residual_input,
    input_norm_gain,
    base_projection_weight,
    query_key_gains,
    adapter_down_weight,
    adapter_up_weight,
    row_adapter_index,
    row_sequence_index,
):
    down = jnp.transpose(adapter_down_weight, (0, 2, 1)).reshape(192, WIDTH)
    up = adapter_up_weight.reshape(64, 4096)
    vm = pl.BlockSpec(memory_space=pltpu.VMEM)
    anyspace = pl.BlockSpec(memory_space=pl.ANY)
    dma = pltpu.SemaphoreType.DMA
    return pl.pallas_call(
        kernel,
        out_shape=jax.ShapeDtypeStruct((ROWS, HEADS * HEAD_DIM), BF16),
        in_specs=[vm] * 8 + [anyspace] * 3,
        out_specs=anyspace,
        scratch_shapes=[
            pltpu.VMEM((2048, WIDTH), BF16),
            pltpu.VMEM((4, 4, 896, 256), BF16),
            pltpu.VMEM((4, 192, WIDTH), BF16),
            pltpu.VMEM((4, 48, 2048), BF16),
            pltpu.VMEM((2, 2048, 256), BF16),
            pltpu.VMEM((2, 2048, 256), BF16),
            pltpu.VMEM((2, 2048, 256), BF16),
            pltpu.VMEM((2048, 512), BF16),
            pltpu.VMEM((2, 1024, 256), F32),
            pltpu.VMEM((2, 1024, 128), F32),
            pltpu.VMEM((4, 8, 128), F32),
            pltpu.VMEM((2, 2, 8, 128), F32),
            pltpu.VMEM((2048, 128), F32),
            pltpu.VMEM((2048, 128), F32),
            pltpu.VMEM((2, 8, 8, 256), F32),
            dma((8,)), dma((2,)), dma((4,)), dma((4,)),
            dma((2, 4)), dma((3, 4)), dma((4,)),
            dma((3,)), dma((4,)),
            dma((4, 4, 2)), dma((4, 4, 2)),
            dma((3, 4)), dma((4, 4)),
            dma((10,)), dma((2, 5)),
            dma((4, 2)), dma((4, 2)),
        ],
        compiler_params=pltpu.CompilerParams(
            collective_id=0, has_side_effects=True, vmem_limit_bytes=60 << 20
        ),
        name="block",
    )(
        residual_input,
        input_norm_gain,
        query_key_gains,
        row_adapter_index.reshape(4, 128),
        row_sequence_index.reshape(4, 128),
        jnp.asarray(FOLD, BF16),
        jnp.asarray(TILE, BF16),
        jnp.asarray(COLS),
        base_projection_weight,
        down,
        up,
    )


def solution(mesh):
    placed = (
        P(("dp", "adapter"), None),
        P(),
        P("adapter", "dp"),
        P(),
        P("adapter", None, None),
        P("adapter", None, None),
        P(("dp", "adapter"), None),
        P(("dp", "adapter")),
    )
    return jax.shard_map(
        body, mesh=mesh, in_specs=placed, out_specs=P(("dp", "adapter"), None), check_vma=False
    )
```

```python
import jax
import jax.numpy as jnp
import numpy as np
from jax import lax
from jax.experimental import pallas as pl
from jax.experimental.pallas import tpu as pltpu
from jax.sharding import PartitionSpec as P

HEADS = 8
KV_HEADS = 4
HEAD_DIM = 256
ROWS = 512
WIDTH = 2560
BF16 = jnp.bfloat16
F32 = jnp.float32


def dot(a, b, dims=((1,), (0,))):
    return lax.dot_general(a, b, (dims, ((), ())), preferred_element_type=F32)


def kernel(
    x_ref, g_ref, gains_ref, aid_ref, sid_ref, fold_ref, tile_ref, cols_ref, w_ref, d_ref, u_ref,
    out_ref,
    xg, wu, dn, rpt, qs, kall, vall, ob, acc_ref, tot_ref, ids, hids, acol, scol, krow,
    sh_send, d_sem, u_sem, w_sem, x_send, x_recv, f_send, i_send, i_recv,
    g_send, g_recv, r_send, r_recv, h_send, h_recv, o_send, o_recv,
):
    dp = lax.axis_index("dp")
    ad = lax.axis_index("adapter")
    x, c = dp // 2, dp % 2
    z, y = ad // 4, ad % 4
    g, yl = y // 2, y % 2

    def dev(x_, c_, z_, y_):
        return (x_ * 2 + c_, z_ * 4 + y_)

    def half_of(y_):
        return ((y_ + 1) // 2) % 2

    def remote(src, dst, ssem, rsem, to):
        return pltpu.make_async_remote_copy(
            src_ref=src, dst_ref=dst, send_sem=ssem, recv_sem=rsem,
            device_id=to, device_id_type=pl.DeviceIdType.MESH,
        )

    def arrived(ref, sem):
        pltpu.make_async_copy(ref, ref, sem).wait()

    half = half_of(y)
    kv = c + 2 * half
    ypar = 1 - 2 * yl + y
    sib = dev(x, 1 - c, z, y)
    mate = dev(x, c, z, ypar)
    diag = dev(x, 1 - c, z, ypar)
    xbit = x // 2
    b = (1 - xbit) * (x % 2) + xbit * c
    px = (1 - xbit) * (1 - x) + xbit * x
    pc = (1 - xbit) * c + xbit * (1 - c)
    up_x, dn_x = (x + 1) % 4, (x + 3) % 4
    up_z, dn_z = (z + 1) % 4, (z + 3) % 4
    y3 = 3 - y
    wrap = g * (z // 3)
    tz = (z + g) % 4
    swrap = (1 - g) * ((3 - z) // 3)
    sz = (z + 3 + g) % 4
    halo_to = [dev(x, c, tz, y3), dev((x + wrap) % 4, c, tz, y3)]
    halo_from = [dev((x + 4 - swrap) % 4, c, sz, y3), dev(x, c, sz, y3)]
    slot_of = [wrap, 1 - wrap]

    barrier = pltpu.get_barrier_semaphore()
    partners = [sib, mate, diag]
    partners += [dev(x, c, z, (y + k) % 4) for k in (1, 2, 3)]
    partners += [dev(px, pc, z, k) for k in range(4)]
    partners += [dev(up_x, c, z, y), dev(dn_x, c, z, y), dev(x, c, up_z, y), dev(x, c, dn_z, y)]
    partners += halo_to + halo_from
    for to in partners:
        pl.semaphore_signal(barrier, inc=1, device_id=to, device_id_type=pl.DeviceIdType.MESH)
    pl.semaphore_wait(barrier, len(partners))

    pending = []

    def go(copy):
        copy.start()
        pending.append(copy)
        return copy

    y2 = (y + 2) % 4
    dsrc = d_ref.at[pl.ds(pl.multiple_of(96 * c, 32), 96), pl.ds(pl.multiple_of(640 * x, 128), 640)]
    ddst = dn.at[z, pl.ds(pl.multiple_of(96 * g, 32), 96), pl.ds(pl.multiple_of(640 * x, 128), 640)]
    dloc = pltpu.make_async_copy(dsrc, ddst, d_sem.at[0])
    dloc.start()
    dsend = go(remote(dsrc, ddst, sh_send.at[0], d_sem.at[1], dev(x, c, z, y2)))

    def up_src(y_):
        kv_ = c + 2 * half_of(y_)
        col = (1 - xbit) * (kv_ * 512 + x * 256) + xbit * (2048 + (x - 2) * 1024 + kv_ * 256)
        return u_ref.at[:, pl.ds(pl.multiple_of(col, 128), 256)]

    udst = wu.at[x, z, pl.ds(pl.multiple_of(640 + 64 * y, 64), 64), :]
    for k in (1, 2, 3):
        yt = (y + k) % 4
        go(remote(up_src(yt), udst, sh_send.at[k], u_sem.at[y], dev(x, c, z, yt)))
    pltpu.make_async_copy(up_src(y), udst, u_sem.at[y]).start()
    kept = w_ref.at[:, pl.ds(pl.multiple_of(b * 256, 256), 256)]
    other = w_ref.at[:, pl.ds(pl.multiple_of((1 - b) * 256, 256), 256)]
    wrows = pl.ds(pl.multiple_of(160 * y, 32), 160)
    kept_sends = []
    for k, yt in enumerate((b, 3 - b)):
        send = remote(kept, wu.at[x, z, wrows, :], sh_send.at[4 + k], w_sem.at[y], dev(x, c, z, yt))
        kept_sends.append((yt, send))

        @pl.when(yt == y)
        def _():
            pltpu.make_async_copy(kept, wu.at[x, z, wrows, :], w_sem.at[y]).start()

        @pl.when(yt != y)
        def _():
            send.start()

        go(remote(other, wu.at[px, z, wrows, :], sh_send.at[6 + k], w_sem.at[y], dev(px, pc, z, yt)))

    own = 2 * c + yl
    ids[own] = jnp.concatenate([aid_ref[...], sid_ref[...]], axis=0).astype(F32)
    for k in range(4):
        val = x_ref[k * 128 : (k + 1) * 128, :].astype(F32)
        scale = lax.rsqrt(jnp.mean(val * val, axis=-1, keepdims=True) + 1e-06)
        rows = pl.ds(pl.multiple_of(own * 512 + k * 128, 128), 128)
        xg[rows, :] = (val * scale * g_ref[...].reshape(1, WIDTH)).astype(BF16)
        go(remote(xg.at[rows, :], xg.at[rows, :], x_send.at[1, k], x_recv.at[1, k], sib))

    for k, to in enumerate((sib, mate, diag)):
        go(remote(ids.at[own], ids.at[own], i_send.at[k], i_recv.at[own], to))

    def block_rows(blk, k):
        return xg.at[pl.ds(pl.multiple_of(blk * 512 + k * 128, 128), 128), :]

    def slot(part, stage, i, lo, n):
        if part < 2:
            rows = pl.ds(part * 96 + lo, n)
            cols_i = pl.ds(pl.multiple_of(i * 640, 128), 640)
            cols_x = pl.ds(pl.multiple_of(x * 640, 128), 640)
            if part == 0:
                return dn.at[z, rows, cols_i] if stage == 0 else dn.at[i, rows, :]
            return dn.at[i, rows, cols_x] if stage == 0 else dn.at[:, rows, cols_i]
        rows = pl.ds((part - 2) * 448 + lo, n)
        if part == 2:
            return wu.at[i, z, rows, :] if stage == 0 else wu.at[:, i, rows, :]
        return wu.at[x, i, rows, :] if stage == 0 else wu.at[i, :, rows, :]

    def step(part, s):
        size = 96 if part < 2 else 448
        stage = s // 2
        along_x = (part % 2 == 0) == (stage == 0)
        me, up, dw = (x, up_x, dn_x) if along_x else (z, up_z, dn_z)
        to_up = dev(up, c, z, y) if along_x else dev(x, c, up, y)
        to_dn = dev(dw, c, z, y) if along_x else dev(x, c, dw, y)
        copies = []
        for way, to in enumerate((to_up, to_dn)):
            if s % 2 == 0:
                ref = slot(part, stage, me, 0, size)
            else:
                ref = slot(part, stage, dw if way == 0 else up, way * (size // 2), size // 2)
            copies.append(
                go(remote(ref, ref, g_send.at[part, s, way], g_recv.at[part, s, way], to))
            )
        return copies

    def done(copies):
        for copy in copies:
            copy.wait_recv()

    dloc.wait()
    dsend.wait_recv()
    d1, d2 = step(0, 0), step(1, 0)
    for k in range(4):
        arrived(wu.at[x, z, pl.ds(640 + 64 * k, 64), :], u_sem.at[k])
        arrived(wu.at[x, z, pl.ds(160 * k, 160), :], w_sem.at[k])
    w1, w2 = step(2, 0), step(3, 0)
    for k in range(4):
        ref = block_rows(own, k)
        go(remote(ref, ref, x_send.at[0, k], x_recv.at[0, k], mate))
    done(d1), done(d2)
    d1, d2 = step(0, 1), step(1, 1)
    done(d1), done(d2)
    d1, d2 = step(0, 2), step(1, 2)
    done(w1), done(w2)
    w1, w2 = step(2, 1), step(3, 1)
    done(d1), done(d2)
    d1, d2 = step(0, 3), step(1, 3)
    done(w1), done(w2)
    w1, w2 = step(2, 2), step(3, 2)

    for k in range(1, 4):
        arrived(ids.at[0], i_recv.at[(own + k) % 4])
    for blk in range(4):
        for k in range(4):
            at = slice(blk * 512 + k * 128, blk * 512 + (k + 1) * 128)
            acol[at, :] = jnp.broadcast_to(ids[blk, k : k + 1, :], (128, 128)).T
            scol[at, :] = jnp.broadcast_to(ids[blk, 4 + k : 5 + k, :], (128, 128)).T
    for r in range(2):
        ref = ids.at[2 * r : 2 * r + 2]
        go(remote(ref, hids.at[slot_of[r]], h_send.at[8 + r], h_recv.at[slot_of[r], 4], halo_to[r]))
    for k in range(4):
        arrived(block_rows(0, 0), x_recv.at[1, k])

    done(d1), done(d2)

    def ranks(o):
        blk = ((c + o) % 2) * 2 + (yl + o // 2) % 2
        rows = pl.ds(pl.multiple_of(blk * 512, 512), 512)
        vals = jnp.concatenate(
            [dot(xg[rows, :], dn[k], ((1,), (1,))).astype(BF16) for k in range(4)], axis=1
        )
        first = (c * 2 + yl * 4).astype(F32)
        mine = acol[rows, 0:1] == cols_ref[0:1, :] + first
        kept_vals = jnp.where(mine, vals.astype(F32), 0.0).astype(BF16)
        rpt[own, :, rows] = dot(fold_ref[...], kept_vals, ((1,), (1,))).astype(BF16)
        for k, to in enumerate((sib, mate, diag)):
            ref = rpt.at[own, :, rows]
            remote(ref, ref, r_send.at[k, o], r_recv.at[own, blk], to).start()

    def two_ranks(first):
        def run(o, carry):
            ranks(o)
            return carry

        lax.fori_loop(first, first + 2, run, 0)

    done(w1), done(w2)
    w1, w2 = step(2, 3), step(3, 3)
    two_ranks(0)
    forwards = []
    mblk = 2 * c + 1 - yl
    for k in range(4):
        arrived(block_rows(0, 0), x_recv.at[0, k])
        ref = block_rows(mblk, k)
        forwards.append(go(remote(ref, ref, f_send.at[k], x_recv.at[2, k], sib)))
    ranks(2)
    done(forwards)
    ranks(3)
    done(w1), done(w2)

    lane = lax.broadcasted_iota(jnp.int32, (1, 128), 1)
    lane_adapter = (lane // 16).astype(F32)

    def halo_copies(blk, o):
        r, part = blk // 2, blk % 2
        src = pl.ds(pl.multiple_of(1024 + part * 512, 512), 512)
        dst = pl.ds(pl.multiple_of(part * 512, 512), 512)
        sl = (r + wrap) % 2
        to = dev((x + wrap * r) % 4, c, tz, y3)
        return [
            remote(buf.at[r, src, :], buf.at[sl, dst, :], h_send.at[2 * o + n],
                   h_recv.at[sl, part * 2 + n], to)
            for n, buf in enumerate((kall, vall))
        ]

    def project(blk, kinds):
        rows = pl.ds(pl.multiple_of(blk * 512, 512), 512)
        total_ranks = rpt[0, :, rows].astype(F32)
        for k in range(1, 4):
            total_ranks = total_ranks + rpt[k, :, rows].astype(F32)
        tiled = dot(total_ranks.T.astype(BF16), tile_ref[...])
        adapters = acol[rows, :]
        for part, col_blocks in kinds:
            mine = tiled[:, part * 128 : (part + 1) * 128]
            spread = [
                jnp.where(adapters == lane_adapter + 8.0 * n, mine, 0.0).astype(BF16)
                for n in range(8)
            ]
            for cb in col_blocks:
                base = jnp.zeros((512, 256), F32)
                delta = jnp.zeros((512, 256), F32)
                for k in range(4):
                    base = base + dot(xg[rows, k * 640 : (k + 1) * 640], wu[cb, k, 0:640, :])
                    pair = jnp.concatenate([spread[2 * k], spread[2 * k + 1]], axis=1)
                    delta = delta + dot(pair, wu[cb, k, 640:896, :])
                proj = base.astype(BF16).astype(F32) + delta.astype(BF16).astype(F32)
                if cb < 3:
                    scale = lax.rsqrt(jnp.mean(proj * proj, axis=-1, keepdims=True) + 1e-06)
                    gain = gains_ref[0:1, :] if cb < 2 else gains_ref[1:2, :]
                    proj = proj * scale * gain
                val = proj.astype(BF16)
                at = pl.ds(pl.multiple_of(1024 + (blk % 2) * 512, 512), 512)
                if cb < 2:
                    qs[cb, rows, :] = val * BF16(0.0625)
                elif cb == 2:
                    kall[blk // 2, at, :] = val
                else:
                    vall[blk // 2, at, :] = val

    def project_kv(o, carry):
        blk = o // 2 * 2 + 1 - o % 2
        for k in range(1, 4):
            src = (own + k) % 4
            arrived(rpt.at[src, :, pl.ds(0, 512)], r_recv.at[src, blk])
        project(blk, ((1, (2,)), (2, (3,))))
        for copy in halo_copies(blk, o):
            copy.start()
        return carry

    def project_q(blk, carry):
        project(blk, ((0, (0, 1)),))
        return carry

    lax.fori_loop(0, 4, project_kv, 0)
    lax.fori_loop(0, 4, project_q, 0)

    for sl in range(2):
        arrived(hids.at[sl], h_recv.at[sl, 4])
    nothing = jnp.where(x * 8 + z * 2 + g == 0, 1.0, 0.0).astype(F32)
    for r in range(2):
        for t in range(8):
            blk, k = (t % 4) // 2, (t % 2) * 2
            if t < 4:
                pair = [hids[r, blk, 4 + k + n : 5 + k + n, :] for n in range(2)]
                if r == 0:
                    pair = [p - nothing * (p + 1.0) for p in pair]
            else:
                pair = [ids[2 * r + blk, 4 + k + n : 5 + k + n, :] for n in range(2)]
            krow[r, t] = jnp.broadcast_to(jnp.concatenate(pair, axis=1), (8, 256))

    ahead = lax.broadcasted_iota(jnp.int32, (256, 256), 0) - lax.broadcasted_iota(
        jnp.int32, (256, 256), 1
    )

    def attend(r, i, h, tiles, acc, total):
        rows = slice(r * 1024 + i * 256, r * 1024 + (i + 1) * 256)
        q = qs[h, rows, :]
        sq = scol[rows, 0:1]
        for t in tiles:
            keys = slice(t * 256, (t + 1) * 256)
            s = dot(q, kall[r, keys, :], ((1,), (1,)))
            ok = sq == krow[r, t, 0:1, :]
            if t == i:
                ok = ok & (ahead < 0)
            if t == i + 4:
                ok = ok & (ahead >= 0)
            w = jnp.where(ok, jnp.exp(s), 0.0)
            more = w[:, 0:128] + w[:, 128:256]
            part = dot(w.astype(BF16), vall[r, keys, :])
            total = more if total is None else total + more
            acc = part if acc is None else acc + part
        return acc, total

    def attend_own(r):
        for i in range(4):
            at = slice(i * 256, (i + 1) * 256)

            def head(h, carry):
                acc, total = attend(r, i, h, range(4, 5 + i), None, None)
                acc_ref[r, h, at, :] = acc
                tot_ref[r, h, at, :] = total
                return carry

            lax.fori_loop(0, 2, head, 0)

    def out_copy(blk, m):
        src = ob.at[pl.ds(blk * 512 + m * 256, 256), :]
        dst = out_ref.at[m * 256 : (m + 1) * 256, pl.ds(pl.multiple_of(kv * 512, 512), 512)]
        return src, dst, dev(x, blk // 2, z, g * 2 + blk % 2)

    def attend_halo(r, part):
        for i in (2 * part + 1, 2 * part):
            at = slice(i * 256, (i + 1) * 256)
            rows = slice(r * 1024 + i * 256, r * 1024 + (i + 1) * 256)

            def head(h, carry):
                acc, total = attend(r, i, h, range(i, 4), acc_ref[r, h, at, :], tot_ref[r, h, at, :])
                norm = jnp.sum(total, axis=-1, keepdims=True)
                ob[rows, pl.ds(pl.multiple_of(h * 256, 256), 256)] = (acc / norm).astype(BF16)
                return carry

            lax.fori_loop(0, 2, head, 0)
            blk, m = 2 * r + part, i % 2
            src, dst, to = out_copy(blk, m)

            @pl.when(blk == own)
            def _():
                pltpu.make_async_copy(src, dst, o_recv.at[own, m]).start()

            @pl.when(blk != own)
            def _():
                remote(src, dst, o_send.at[blk, m], o_recv.at[own, m], to).start()

    attend_own(0)
    attend_own(1)
    for r in range(2):
        for part in (1, 0):
            for n in range(2):
                arrived(kall.at[r, pl.ds(0, 512), :], h_recv.at[r, 2 * part + n])
            attend_halo(r, part)

    for k in range(4):
        for m in range(2):
            arrived(out_ref.at[0:256, pl.ds(0, 512)], o_recv.at[k, m])
    for blk in range(4):

        @pl.when(blk != own)
        def _():
            for m in range(2):
                src, dst, to = out_copy(blk, m)
                remote(src, dst, o_send.at[blk, m], o_recv.at[own, m], to).wait_send()

    for o in range(4):
        for k, to in enumerate((sib, mate, diag)):
            ref = rpt.at[own, :, pl.ds(0, 512)]
            remote(ref, ref, r_send.at[k, o], r_recv.at[own, o], to).wait_send()
        blk = o // 2 * 2 + 1 - o % 2
        for copy in halo_copies(blk, o):
            copy.wait_send()
    for yt, send in kept_sends:

        @pl.when(yt != y)
        def _():
            send.wait_send()

    for copy in pending:
        copy.wait_send()


FOLD = np.zeros((48, 768), np.float32)
FOLD[np.arange(768) % 48, np.arange(768)] = 1.0
TILE = np.zeros((48, 384), np.float32)
for _lane in range(384):
    TILE[(_lane // 128) * 16 + _lane % 16, _lane] = 1.0
_c = np.arange(768)
COLS = np.tile(((_c // 192) * 16 + (_c % 192 // 96) * 8 + _c % 96 // 48).astype(np.float32), (8, 1))


def body(
    residual_input,
    input_norm_gain,
    base_projection_weight,
    query_key_gains,
    adapter_down_weight,
    adapter_up_weight,
    row_adapter_index,
    row_sequence_index,
):
    down = jnp.transpose(adapter_down_weight, (0, 2, 1)).reshape(192, WIDTH)
    up = adapter_up_weight.reshape(64, 4096)
    vm = pl.BlockSpec(memory_space=pltpu.VMEM)
    anyspace = pl.BlockSpec(memory_space=pl.ANY)
    dma = pltpu.SemaphoreType.DMA
    return pl.pallas_call(
        kernel,
        out_shape=jax.ShapeDtypeStruct((ROWS, HEADS * HEAD_DIM), BF16),
        in_specs=[vm] * 8 + [anyspace] * 3,
        out_specs=anyspace,
        scratch_shapes=[
            pltpu.VMEM((2048, WIDTH), BF16),
            pltpu.VMEM((4, 4, 896, 256), BF16),
            pltpu.VMEM((4, 192, WIDTH), BF16),
            pltpu.VMEM((4, 48, 2048), BF16),
            pltpu.VMEM((2, 2048, 256), BF16),
            pltpu.VMEM((2, 2048, 256), BF16),
            pltpu.VMEM((2, 2048, 256), BF16),
            pltpu.VMEM((2048, 512), BF16),
            pltpu.VMEM((2, 2, 1024, 256), F32),
            pltpu.VMEM((2, 2, 1024, 128), F32),
            pltpu.VMEM((4, 8, 128), F32),
            pltpu.VMEM((2, 2, 8, 128), F32),
            pltpu.VMEM((2048, 128), F32),
            pltpu.VMEM((2048, 128), F32),
            pltpu.VMEM((2, 8, 8, 256), F32),
            dma((8,)), dma((2,)), dma((4,)), dma((4,)),
            dma((2, 4)), dma((3, 4)), dma((4,)),
            dma((3,)), dma((4,)),
            dma((4, 4, 2)), dma((4, 4, 2)),
            dma((3, 4)), dma((4, 4)),
            dma((10,)), dma((2, 5)),
            dma((4, 2)), dma((4, 2)),
        ],
        compiler_params=pltpu.CompilerParams(
            collective_id=0, has_side_effects=True, vmem_limit_bytes=60 << 20
        ),
        name="block",
    )(
        residual_input,
        input_norm_gain,
        query_key_gains,
        row_adapter_index.reshape(4, 128),
        row_sequence_index.reshape(4, 128),
        jnp.asarray(FOLD, BF16),
        jnp.asarray(TILE, BF16),
        jnp.asarray(COLS),
        base_projection_weight,
        down,
        up,
    )


def solution(mesh):
    placed = (
        P(("dp", "adapter"), None),
        P(),
        P("adapter", "dp"),
        P(),
        P("adapter", None, None),
        P("adapter", None, None),
        P(("dp", "adapter"), None),
        P(("dp", "adapter")),
    )
    return jax.shard_map(
        body, mesh=mesh, in_specs=placed, out_specs=P(("dp", "adapter"), None), check_vma=False
    )
```
